256 devices in a mesh: tm: 16 (over z, core), pts: 16 (over x, y).
Axes of the slice: x: 4, y: 4, z: 8, core: 2. Of those that a mesh axis runs over, the one named last changes fastest.
Arguments:
- snapshots: float32 [1024, 131072], P('tm', 'pts'), may hold values from -110 to 110
- weights: float32 [131072], P(('pts', 'tm')), may hold values from 0.25 to 12, as said below
Outputs:
- modes: float32 [2, 33, 31, 131072], P(None, None, None, ('pts', 'tm'))
- triangle: float32 [2, 33, 31, 31], replicated
The draws below stay inside these ranges and needn't reach their ends.
Inputs may be any that keep to these rules, and one draw needn't show every extreme that they name: Positive weights.
All inputs are finite; a program needn't handle non-finite values.
Results may differ from the reference program's by a relative error of at most 0.00065.
Values sent between devices are 32-bit elements; how exact they have to be, the bound alone decides.
A program may use at most 128 MiB of HBM per device.

```python
import math
import jax
import jax.numpy as jnp
from jax import lax

SEG = 64
HOP = 32
NF = 33
NT = 1024
NB = 31
NP = 131072


def draw_snapshots(key, part):
    key_noise, key_time, key_point, key_coef, key_shape = jax.random.split(key, 5)
    noise_level = 0.0004 * math.sqrt(NB)
    coefficient = jnp.clip(jax.random.normal(key_coef, (NT, 8), jnp.float32), -2.5, 2.5)
    pattern = jnp.clip(jax.random.normal(key_shape, (8, NP), jnp.float32), -2.5, 2.5)
    noise_part = jnp.clip(jax.random.normal(key_noise, (NT, NP), jnp.float32), -4.0, 4.0)
    time_scale = jnp.exp(jax.random.uniform(key_time, (NT, 1), jnp.float32, math.log(0.5), math.log(2.0)))
    point_scale = jnp.exp(jax.random.uniform(key_point, (1, NP), jnp.float32, 0.0, math.log(10.0)))
    values = jnp.zeros((NT, NP), jnp.float32)
    for mode_number in range(8):
        amplitude = 0.25 * math.exp(-math.log(10.0) * mode_number / 7.0)
        values = values + amplitude * coefficient[:, mode_number:mode_number + 1] * pattern[mode_number:mode_number + 1, :]
    values = (values + noise_level * noise_part) * time_scale * point_scale
    return values.astype(jnp.float32)


def draw_weights(key, part):
    trend = 1.0 + 2.0 * jnp.arange(NP).astype(jnp.float32) / NP
    rough = jnp.exp(jax.random.uniform(key, (NP,), jnp.float32, math.log(0.5), math.log(2.0)))
    return (trend * rough).astype(jnp.float32)


def setup_inputs(seed: int = 0) -> dict:
    streams_of = jax.random.split(jax.random.key(seed), 3)
    return {
        "snapshots": draw_snapshots(jax.random.fold_in(streams_of[2], 71), 0),
        "weights": draw_weights(jax.random.fold_in(streams_of[2], 71), 0),
    }


EXACT = lax.Precision.HIGHEST

def fourier_table():
    sample = jnp.arange(SEG).astype(jnp.float32)[:, None]
    column = jnp.arange(SEG)[None, :]
    frequency = jnp.where(column < NF, column, column - HOP).astype(jnp.float32)
    window = 0.5 - 0.5 * jnp.cos(2.0 * math.pi * sample / SEG)
    phase_angle = 2.0 * math.pi * frequency * sample / SEG
    waveform = jnp.where(column < NF, jnp.cos(phase_angle), -jnp.sin(phase_angle))
    return waveform * window / jnp.sqrt(jnp.float32(3 * SEG / 8))

def split_spectrum(spectrum):
    padding = jnp.zeros((1,) + spectrum.shape[1:], spectrum.dtype)
    part_real = spectrum[:NF]
    part_imag = jnp.concatenate([padding, spectrum[NF:], padding], axis=0)
    return (part_real, part_imag)

def gram(left_real, left_imag):

    def contract(first, second):
        return jnp.einsum('fbp,fcp->fbc', first, second, precision=EXACT)
    return (contract(left_real, left_real) + contract(left_imag, left_imag), contract(left_real, left_imag) - contract(left_imag, left_real))

def cholesky_upper(gram_real, gram_imag):
    width = gram_real.shape[-1]
    position = jnp.arange(width)

    def advance(k, loop_state):
        work_real, work_imag, upper_real, upper_imag = loop_state
        pivot_real = lax.dynamic_index_in_dim(work_real, k, axis=1, keepdims=False)
        pivot_imag = lax.dynamic_index_in_dim(work_imag, k, axis=1, keepdims=False)
        pivot = jnp.sqrt(lax.dynamic_index_in_dim(pivot_real, k, axis=1, keepdims=False))
        keep_mask = (position >= k)[None, :]
        pivot_real = jnp.where(keep_mask, pivot_real / pivot[:, None], 0.0)
        pivot_imag = jnp.where(keep_mask, pivot_imag / pivot[:, None], 0.0)
        upper_real = lax.dynamic_update_index_in_dim(upper_real, pivot_real, k, axis=1)
        upper_imag = lax.dynamic_update_index_in_dim(upper_imag, pivot_imag, k, axis=1)
        work_real = work_real - (pivot_real[:, :, None] * pivot_real[:, None, :] + pivot_imag[:, :, None] * pivot_imag[:, None, :])
        work_imag = work_imag - (pivot_real[:, :, None] * pivot_imag[:, None, :] - pivot_imag[:, :, None] * pivot_real[:, None, :])
        return (work_real, work_imag, upper_real, upper_imag)
    start = (gram_real, gram_imag, jnp.zeros_like(gram_real), jnp.zeros_like(gram_imag))
    result = lax.fori_loop(0, width, advance, start)
    return (result[2], result[3])

def invert_upper(upper_real, upper_imag):
    width = upper_real.shape[-1]
    position = jnp.arange(width)

    def advance(i, loop_state):
        inverse_real, inverse_imag = loop_state
        k = width - 1 - i
        row_real = lax.dynamic_index_in_dim(upper_real, k, axis=1, keepdims=False)
        row_imag = lax.dynamic_index_in_dim(upper_imag, k, axis=1, keepdims=False)
        pivot = lax.dynamic_index_in_dim(row_real, k, axis=1, keepdims=False)

        def contract(first, second):
            return jnp.einsum('fj,fjc->fc', first, second, precision=EXACT)
        sum_real = contract(row_real, inverse_real) - contract(row_imag, inverse_imag)
        sum_imag = contract(row_real, inverse_imag) + contract(row_imag, inverse_real)
        unit_row = (position == k).astype(upper_real.dtype)[None, :]
        new_real = (unit_row - sum_real) / pivot[:, None]
        new_imag = -sum_imag / pivot[:, None]
        inverse_real = lax.dynamic_update_index_in_dim(inverse_real, new_real, k, axis=1)
        inverse_imag = lax.dynamic_update_index_in_dim(inverse_imag, new_imag, k, axis=1)
        return (inverse_real, inverse_imag)
    return lax.fori_loop(0, width, advance, (jnp.zeros_like(upper_real), jnp.zeros_like(upper_imag)))

def apply_inverse(basis_real, basis_imag, inverse_real, inverse_imag):

    def contract(first, second):
        return jnp.einsum('fbc,fbp->fcp', first, second, precision=EXACT)
    return (contract(inverse_real, basis_real) - contract(inverse_imag, basis_imag), contract(inverse_real, basis_imag) + contract(inverse_imag, basis_real))

def product_upper(left_real, left_imag, right_real, right_imag):

    def contract(first, second):
        return jnp.einsum('fbj,fjc->fbc', first, second, precision=EXACT)
    return (contract(left_real, right_real) - contract(left_imag, right_imag), contract(left_real, right_imag) + contract(left_imag, right_real))

def factorize(basis_real, basis_imag):
    gram_real, gram_imag = gram(basis_real, basis_imag)
    upper_real, upper_imag = cholesky_upper(gram_real / NP, gram_imag / NP)
    inverse_real, inverse_imag = invert_upper(upper_real, upper_imag)
    ortho_real, ortho_imag = apply_inverse(basis_real, basis_imag, inverse_real, inverse_imag)
    return (ortho_real, ortho_imag, upper_real, upper_imag)

def reference(snapshots, weights):
    hop_rows = snapshots.reshape(NT // HOP, HOP, snapshots.shape[1])
    blocks = jnp.concatenate([hop_rows[:-1], hop_rows[1:]], axis=1)
    spectrum = jnp.einsum('bnp,nc->cbp', blocks, fourier_table(), precision=EXACT)
    part_real, part_imag = split_spectrum(spectrum)
    root_weight = jnp.sqrt(weights)[None, None, :]
    first_real, first_imag, upper1_real, upper1_imag = factorize(part_real * root_weight, part_imag * root_weight)
    final_real, final_imag, upper2_real, upper2_imag = factorize(first_real, first_imag)
    total_real, total_imag = product_upper(upper2_real, upper2_imag, upper1_real, upper1_imag)
    return (jnp.stack([final_real, final_imag]), jnp.stack([total_real, total_imag]))
```

```python
import math

import jax
import jax.numpy as jnp
from jax import lax
from jax.experimental import pallas as pl
from jax.experimental.pallas import tpu as pltpu
from jax.sharding import PartitionSpec as P

SEG = 64
HOP = 32
NF = 33
NT = 1024
NB = 31
MESH = pl.DeviceIdType.MESH

EXACT = lax.Precision.HIGHEST


def fourier_table():
    sample = jnp.arange(SEG).astype(jnp.float32)[:, None]
    column = jnp.arange(SEG)[None, :]
    frequency = jnp.where(column < NF, column, column - HOP).astype(jnp.float32)
    window = 0.5 - 0.5 * jnp.cos(2.0 * math.pi * sample / SEG)
    phase_angle = 2.0 * math.pi * frequency * sample / SEG
    waveform = jnp.where(column < NF, jnp.cos(phase_angle), -jnp.sin(phase_angle))
    return waveform * window / jnp.sqrt(jnp.float32(3 * SEG / 8))


def split_spectrum(spectrum):
    padding = jnp.zeros((1,) + spectrum.shape[1:], spectrum.dtype)
    part_real = spectrum[:NF]
    part_imag = jnp.concatenate([padding, spectrum[NF:], padding], axis=0)
    return (part_real, part_imag)


def gram(left_real, left_imag):

    def contract(first, second):
        return jnp.einsum("fbp,fcp->fbc", first, second, precision=EXACT)

    return (
        contract(left_real, left_real) + contract(left_imag, left_imag),
        contract(left_real, left_imag) - contract(left_imag, left_real),
    )


def apply_inverse(basis_real, basis_imag, inverse_real, inverse_imag):

    def contract(first, second):
        return jnp.einsum("fcb,fbp->fcp", first, second, precision=EXACT)

    return (
        contract(inverse_real, basis_real) - contract(inverse_imag, basis_imag),
        contract(inverse_real, basis_imag) + contract(inverse_imag, basis_real),
    )


def product_upper(left_real, left_imag, right_real, right_imag):

    def contract(first, second):
        return jnp.einsum("fbj,fjc->fbc", first, second, precision=EXACT)

    return (
        contract(left_real, right_real) - contract(left_imag, right_imag),
        contract(left_real, right_imag) + contract(left_imag, right_real),
    )


def pack_gram(gram_real, gram_imag):
    pad = ((0, 0), (0, 1), (0, 1))
    gram_real = jnp.pad(gram_real, pad)
    gram_imag = jnp.pad(gram_imag, pad)
    row = jnp.arange(32)[:, None]
    column = jnp.arange(32)[None, :]
    upper = column >= row
    tiles = jnp.where(upper, gram_real[:32], gram_imag[:32])
    moved = jnp.concatenate([gram_real[32, 31:], gram_real[32, :31]], axis=0)
    first = jnp.where(upper, gram_real[0], moved)
    tiles = jnp.concatenate([first[None], tiles[1:]], axis=0)
    return tiles.reshape(8, 4, 32, 32).transpose(0, 2, 1, 3).reshape(16, 16, 128)


def unpack_gram(packed, points_total):
    tiles = packed.reshape(8, 32, 4, 32).transpose(1, 3, 0, 2).reshape(32, 32, 32)
    tiles = tiles * (1.0 / points_total)
    turned = jnp.swapaxes(tiles, 0, 1)
    row = jnp.arange(32)[:, None, None]
    column = jnp.arange(32)[None, :, None]
    gram_real = jnp.where(column >= row, tiles, turned)
    gram_imag = jnp.where(column < row, tiles, jnp.where(column > row, -turned, 0.0))
    first = jnp.arange(32)[None, None, :] == 0
    gram_imag = jnp.where(first, 0.0, gram_imag)
    lower = jnp.pad(tiles[1:, :, :1], ((0, 1), (0, 0), (0, 0)))
    last = jnp.where(column <= row, lower, jnp.swapaxes(lower, 0, 1))
    gram_real = jnp.concatenate([gram_real, last], axis=2)
    gram_imag = jnp.concatenate([gram_imag, jnp.zeros_like(last)], axis=2)
    return (gram_real[:NB], gram_imag[:NB])


def sum_kernel(n, x_ref, o_ref, part, total, share, send1, recv1, send2, recv2, send3, recv3):
    me_p = lax.axis_index("pts")
    me_t = lax.axis_index("tm")

    def ahead(me, d):
        return lax.rem(me + d, n)

    def scatter(d):
        to = ahead(me_p, d)
        return pltpu.make_async_remote_copy(
            src_ref=x_ref.at[to],
            dst_ref=part.at[d],
            send_sem=send1.at[d],
            recv_sem=recv1.at[d],
            device_id={"pts": to},
            device_id_type=MESH,
        )

    def exchange(d):
        return pltpu.make_async_remote_copy(
            src_ref=total,
            dst_ref=share.at[me_t],
            send_sem=send2.at[d],
            recv_sem=recv2.at[d],
            device_id={"tm": ahead(me_t, d)},
            device_id_type=MESH,
        )

    def gather(d):
        return pltpu.make_async_remote_copy(
            src_ref=total,
            dst_ref=o_ref.at[me_p],
            send_sem=send3.at[d],
            recv_sem=recv3.at[d],
            device_id={"pts": ahead(me_p, d)},
            device_id_type=MESH,
        )

    def each(action):
        def step(d, carry):
            action(d)
            return carry

        lax.fori_loop(1, n, step, 0)

    barrier = pltpu.get_barrier_semaphore()

    def greet(d):
        pl.semaphore_signal(
            barrier, inc=1, device_id={"pts": ahead(me_p, d)}, device_id_type=MESH
        )
        pl.semaphore_signal(
            barrier, inc=1, device_id={"tm": ahead(me_t, d)}, device_id_type=MESH
        )

    each(greet)
    pl.semaphore_wait(barrier, 2 * (n - 1))

    each(lambda d: scatter(d).start())
    part[0] = x_ref[me_p]
    each(lambda d: scatter(d).wait_recv())
    total[...] = jnp.sum(part[...], axis=0)
    each(lambda d: exchange(d).start())
    share[me_t] = total[...]
    each(lambda d: exchange(d).wait())
    total[...] = jnp.sum(share[...], axis=0)
    each(lambda d: gather(d).start())
    o_ref[me_p] = total[...]
    each(lambda d: scatter(d).wait_send())
    each(lambda d: gather(d).wait())


def global_sum(packed):
    n = packed.shape[0]
    vmem = pl.BlockSpec(memory_space=pltpu.VMEM)
    return pl.pallas_call(
        lambda *refs: sum_kernel(n, *refs),
        out_shape=jax.ShapeDtypeStruct(packed.shape, packed.dtype),
        in_specs=[vmem],
        out_specs=vmem,
        scratch_shapes=[
            pltpu.VMEM(packed.shape, jnp.float32),
            pltpu.VMEM(packed.shape[1:], jnp.float32),
            pltpu.VMEM(packed.shape, jnp.float32),
        ]
        + [pltpu.SemaphoreType.DMA((n,))] * 6,
        compiler_params=pltpu.CompilerParams(collective_id=0, has_side_effects=True),
        name="global_sum",
    )(packed)


def factor_kernel(gram_real, gram_imag, out_real, out_imag):
    width, columns, lanes = gram_real.shape
    out_real[...] = gram_real[...]
    out_imag[...] = gram_imag[...]
    column = lax.broadcasted_iota(jnp.int32, (columns, lanes), 0)
    for k in range(width):
        here = column == k
        inverse = 1.0 / jnp.sqrt(out_real[k, k : k + 1, :])
        row_real = jnp.where(here, inverse, out_real[k] * inverse)
        row_imag = jnp.where(here, 0.0, out_imag[k] * inverse)
        out_real[k] = row_real
        out_imag[k] = row_imag

        def eliminate(i, carry):
            pick_real = out_real[k, pl.ds(i, 1), :]
            pick_imag = out_imag[k, pl.ds(i, 1), :]
            work_real = jnp.where(here, 0.0, out_real[i])
            work_imag = jnp.where(here, 0.0, out_imag[i])
            out_real[i] = work_real - (pick_real * row_real + pick_imag * row_imag)
            out_imag[i] = work_imag - (pick_real * row_imag - pick_imag * row_real)
            return carry

        lax.fori_loop(k + 1, width, eliminate, 0, unroll=True)


def factor(gram_real, gram_imag):
    vmem = pl.BlockSpec(memory_space=pltpu.VMEM)
    shape = jax.ShapeDtypeStruct(gram_real.shape, gram_real.dtype)
    return pl.pallas_call(
        factor_kernel,
        out_shape=(shape, shape),
        in_specs=[vmem, vmem],
        out_specs=(vmem, vmem),
        name="factor",
    )(gram_real, gram_imag)


def split_factor(mixed_real, mixed_imag):
    mixed_real = jnp.transpose(mixed_real[:, :NB], (2, 0, 1))
    mixed_imag = jnp.transpose(mixed_imag[:, :NB], (2, 0, 1))
    row = jnp.arange(NB)[:, None]
    column = jnp.arange(NB)[None, :]
    upper_real = jnp.where(
        column > row, mixed_real, jnp.where(column == row, 1.0 / mixed_real, 0.0)
    )
    upper_imag = jnp.where(column > row, mixed_imag, 0.0)
    turned_real = jnp.where(column <= row, mixed_real, 0.0)
    turned_imag = jnp.where(column < row, -mixed_imag, 0.0)
    return upper_real, upper_imag, turned_real, turned_imag


def factorize(basis_real, basis_imag, points_total):
    packed = global_sum(pack_gram(*gram(basis_real, basis_imag)))
    mixed = factor(*unpack_gram(packed, points_total))
    upper_real, upper_imag, turned_real, turned_imag = split_factor(*mixed)
    ortho_real, ortho_imag = apply_inverse(basis_real, basis_imag, turned_real, turned_imag)
    return (ortho_real, ortho_imag, upper_real, upper_imag)


def shards(snapshots, weights):
    records = lax.all_to_all(snapshots, "tm", split_axis=1, concat_axis=0, tiled=True)
    hop_rows = records.reshape(NT // HOP, HOP, records.shape[1])
    blocks = jnp.concatenate([hop_rows[:-1], hop_rows[1:]], axis=1)
    spectrum = jnp.einsum("bnp,nc->cbp", blocks, fourier_table(), precision=EXACT)
    part_real, part_imag = split_spectrum(spectrum)
    points_total = weights.shape[0] * lax.axis_size("tm") * lax.axis_size("pts")
    root_weight = jnp.sqrt(weights)[None, None, :]
    first_real, first_imag, upper1_real, upper1_imag = factorize(
        part_real * root_weight, part_imag * root_weight, points_total
    )
    final_real, final_imag, upper2_real, upper2_imag = factorize(
        first_real, first_imag, points_total
    )
    total_real, total_imag = product_upper(upper2_real, upper2_imag, upper1_real, upper1_imag)
    return (jnp.stack([final_real, final_imag]), jnp.stack([total_real, total_imag]))


def solution(mesh):
    placed = (P("tm", "pts"), P(("pts", "tm")))
    return jax.shard_map(
        shards,
        mesh=mesh,
        in_specs=placed,
        out_specs=(P(None, None, None, ("pts", "tm")), P()),
        check_vma=False,
    )
```

```python
import jax
import jax.numpy as jnp
import ml_dtypes
import numpy as np
from jax import lax
from jax.experimental import pallas as pl
from jax.experimental.pallas import tpu as pltpu
from jax.sharding import PartitionSpec as P

SEG = 64
HOP = 32
NF = 33
NT = 1024
NB = 31
MESH = pl.DeviceIdType.MESH

VMEM = pl.BlockSpec(memory_space=pltpu.VMEM)
TILE = 32
SLOTS = 32


def fourier_table():
    sample = np.arange(SEG)[:, None]
    column = np.arange(SEG)[None, :]
    frequency = np.where(column < NF, column, column - HOP)
    window = 0.5 - 0.5 * np.cos(2.0 * np.pi * sample / SEG)
    phase_angle = 2.0 * np.pi * ((frequency * sample) % SEG) / SEG
    waveform = np.where(column < NF, np.cos(phase_angle), -np.sin(phase_angle))
    return (waveform * window / np.sqrt(3 * SEG / 8)).astype(np.float32)


def table_parts():
    table = fourier_table().T
    high = table.astype(ml_dtypes.bfloat16)
    rest = table - high.astype(np.float32)
    middle = rest.astype(ml_dtypes.bfloat16)
    low = (rest - middle.astype(np.float32)).astype(ml_dtypes.bfloat16)
    return np.concatenate([high, high, middle, high, middle, low], axis=1)


def parts_of(value, count):
    parts = []
    for _ in range(count):
        part = value.astype(jnp.bfloat16)
        parts.append(part)
        value = value - part.astype(jnp.float32)
    return parts


def left6(value):
    high, middle, low = parts_of(value, 3)
    return jnp.concatenate([high, high, middle, high, middle, low], axis=1)


def right6(value):
    high, middle, low = parts_of(value, 3)
    return jnp.concatenate([high, middle, high, low, middle, high], axis=0)


def left3(value):
    high, low = parts_of(value, 2)
    return jnp.concatenate([high, high, low], axis=1)


def right3(value):
    high, low = parts_of(value, 2)
    return jnp.concatenate([high, low, high], axis=0)


def multiply(left, right):
    return jnp.dot(left, right, preferred_element_type=jnp.float32)


def self_product(value, count):
    stacked = jnp.concatenate(parts_of(value, count), axis=0)
    whole = lax.dot_general(
        stacked, stacked, (((1,), (1,)), ((), ())), preferred_element_type=jnp.float32
    )
    size = value.shape[0]
    rows = sum(whole[i * size : (i + 1) * size] for i in reversed(range(count)))
    return sum(rows[:, i * size : (i + 1) * size] for i in reversed(range(count)))


def gram_tile(product, slot):
    top_left = product[:TILE, :TILE]
    bottom_right = product[TILE:, TILE:]
    row = lax.broadcasted_iota(jnp.int32, (TILE, TILE), 0)
    column = lax.broadcasted_iota(jnp.int32, (TILE, TILE), 1)
    if slot == 0:
        return jnp.where(column >= row, top_left, pltpu.roll(bottom_right, 1, 0))
    imaginary = product[:TILE, TILE:] - product[TILE:, :TILE]
    return jnp.where(column >= row, top_left + bottom_right, imaginary)


def put_tiles(out, group, tiles):
    joined = jnp.concatenate(tiles, axis=1)
    out[2 * group] = joined[:16]
    out[2 * group + 1] = joined[16:]


def slot_rows(spectrum, slot):
    halves = [
        [
            spectrum[panel, pl.ds(slot + half, TILE, stride=SEG), :]
            for panel in range(spectrum.shape[0])
        ]
        for half in (0, 32)
    ]
    return jnp.concatenate([jnp.concatenate(row, axis=1) for row in halves], axis=0)


def spectrum_kernel(records, weights, table, spectrum, packed):
    root = jnp.sqrt(weights[...])

    def block(b, carry):
        rows = records[pl.ds(pl.multiple_of(HOP * b, HOP), SEG), :]
        lines = pl.ds(pl.multiple_of(SEG * b, SEG), SEG)
        value = multiply(table[...], right6(rows)) * root
        for panel in range(spectrum.shape[0]):
            spectrum[panel, lines, :] = value[:, 128 * panel : 128 * (panel + 1)]
        return carry

    lax.fori_loop(0, NB, block, 0, unroll=True)
    for panel in range(spectrum.shape[0]):
        spectrum[panel, NB * SEG :, :] = jnp.zeros((SEG, 128), jnp.float32)
    for group in range(8):
        tiles = []
        for slot in range(group, SLOTS, 8):
            value = slot_rows(spectrum, slot)
            tiles.append(gram_tile(self_product(value, 3), slot))
        put_tiles(packed, group, tiles)


def spectra(records, weights):
    points = records.shape[1]
    return pl.pallas_call(
        spectrum_kernel,
        out_shape=(
            jax.ShapeDtypeStruct((points // 128, TILE * SEG, 128), jnp.float32),
            jax.ShapeDtypeStruct((16, 16, 128), jnp.float32),
        ),
        in_specs=[VMEM] * 3,
        out_specs=(VMEM, VMEM),
        compiler_params=pltpu.CompilerParams(vmem_limit_bytes=48 << 20),
        name="spectra",
    )(records, weights.reshape(1, points), jnp.asarray(table_parts()))


def sum_kernel(x_ref, o_ref, half, part, total, share, full, *sems):
    send0, recv0, send1, recv1, send2, recv2, send3, recv3, send4, recv4 = sems
    me_p = lax.axis_index("pts")
    me_t = lax.axis_index("tm")
    core = lax.rem(me_t, 2)
    chip = me_t // 2
    n = part.shape[0]
    chips = share.shape[0]
    other = {"tm": me_t + 1 - 2 * core}
    own_lines = pl.ds(pl.multiple_of(8 * core, 8), 8)
    other_lines = pl.ds(pl.multiple_of(8 - 8 * core, 8), 8)

    def ahead(d):
        return lax.rem(me_p + d, n)

    def remote(source, target, send, recv, device):
        return pltpu.make_async_remote_copy(
            src_ref=source, dst_ref=target, send_sem=send, recv_sem=recv,
            device_id=device, device_id_type=MESH,
        )

    def along(d):
        return {"tm": lax.rem(me_t + 2 * d, 2 * chips)}

    swap = remote(x_ref.at[:, other_lines, :], half, send0, recv0, other)

    def scatter(d):
        return remote(
            full.at[ahead(d)], part.at[d], send1.at[d], recv1.at[d], {"pts": ahead(d)}
        )

    def exchange(d):
        return remote(total, share.at[chip], send2.at[d], recv2.at[d], along(d))

    def gather(d):
        return remote(
            total, o_ref.at[me_p, own_lines, :], send3.at[d], recv3.at[d], {"pts": ahead(d)}
        )

    back = remote(
        o_ref.at[:, own_lines, :], o_ref.at[:, own_lines, :], send4, recv4, other
    )

    def each(count, action):
        def step(d, carry):
            action(d)
            return carry

        lax.fori_loop(1, count, step, 0)

    barrier = pltpu.get_barrier_semaphore()

    def greet(device):
        pl.semaphore_signal(barrier, inc=1, device_id=device, device_id_type=MESH)

    greet(other)
    each(n, lambda d: greet({"pts": ahead(d)}))
    each(chips, lambda d: greet(along(d)))
    pl.semaphore_wait(barrier, n + chips - 1)

    swap.start()
    swap.wait()
    full[...] = x_ref[:, own_lines, :] + half[...]
    each(n, lambda d: scatter(d).start())
    part[0] = full[me_p]
    each(n, lambda d: scatter(d).wait())
    total[...] = jnp.sum(part[...], axis=0)
    each(chips, lambda d: exchange(d).start())
    share[chip] = total[...]
    each(chips, lambda d: exchange(d).wait())
    total[...] = jnp.sum(share[...], axis=0)
    each(n, lambda d: gather(d).start())
    o_ref[me_p, own_lines, :] = total[...]
    each(n, lambda d: gather(d).wait())
    back.start()
    back.wait()


def global_sum(packed):
    n, lines, lanes = packed.shape
    chips = lax.axis_size("tm") // 2
    dma = pltpu.SemaphoreType.DMA
    buffer = pltpu.VMEM((n, lines // 2, lanes), jnp.float32)
    return pl.pallas_call(
        sum_kernel,
        out_shape=jax.ShapeDtypeStruct(packed.shape, packed.dtype),
        in_specs=[VMEM],
        out_specs=VMEM,
        scratch_shapes=[
            buffer,
            buffer,
            pltpu.VMEM((lines // 2, lanes), jnp.float32),
            pltpu.VMEM((chips, lines // 2, lanes), jnp.float32),
            buffer,
            dma, dma, dma((n,)), dma((n,)), dma((chips,)), dma((chips,)),
            dma((n,)), dma((n,)), dma, dma,
        ],
        compiler_params=pltpu.CompilerParams(collective_id=0, has_side_effects=True),
        name="global_sum",
    )(packed)


def factor_lanes(scale, packed, tiles, state_real, state_imag):
    column = lax.broadcasted_iota(jnp.int32, (TILE, 128), 0)
    lane = lax.broadcasted_iota(jnp.int32, (TILE, 128), 1)
    for b in range(TILE):
        lines = packed[pl.ds(b, 8, stride=TILE), :]
        spread = jnp.concatenate(
            [lines] + [pltpu.roll(lines, 128 - 32 * s, 1) for s in (1, 2, 3)]
            + [jnp.zeros((96, 128), jnp.float32)],
            axis=0,
        )
        tiles[b * TILE : (b + 1) * TILE, :] = jnp.transpose(spread)[:TILE] * scale
    tiles[TILE * TILE :, :] = jnp.zeros((TILE, 128), jnp.float32)
    for b in range(NB):
        straight = tiles[b * TILE : (b + 1) * TILE, :]
        turned = tiles[pl.ds(b, TILE, stride=TILE), :]
        below = tiles[(b + 1) * TILE : (b + 2) * TILE, :]
        below_turned = tiles[pl.ds(TILE + b, TILE, stride=TILE), :]
        last = pltpu.roll(jnp.where(column <= b, below, below_turned), 32, 1)
        real = jnp.where(column >= b, straight, turned)
        real = jnp.where(lane == 32, last, real)
        imag = jnp.where(column < b, straight, -turned)
        state_real[b] = jnp.where(lane > 32, jnp.where(column == b, 1.0, 0.0), real)
        state_imag[b] = jnp.where(
            (lane == 0) | (lane >= 32) | (column == b), 0.0, imag
        )
    for k in range(NB):
        here = column == k
        inverse = 1.0 / jnp.sqrt(state_real[k, k : k + 1, :])
        row_real = jnp.where(here, inverse, state_real[k] * inverse)
        row_imag = jnp.where(here, 0.0, state_imag[k] * inverse)
        state_real[k] = row_real
        state_imag[k] = row_imag

        def eliminate(i, carry):
            pick_real = state_real[k, pl.ds(i, 1), :]
            pick_imag = state_imag[k, pl.ds(i, 1), :]
            work_real = jnp.where(here, 0.0, state_real[i])
            work_imag = jnp.where(here, 0.0, state_imag[i])
            state_real[i] = work_real - (pick_real * row_real + pick_imag * row_imag)
            state_imag[i] = work_imag - (pick_real * row_imag - pick_imag * row_real)
            return carry

        lax.fori_loop(k + 1, NB, eliminate, 0, unroll=True)


def write_inverse(state_real, state_imag, inverse):
    column = lax.broadcasted_iota(jnp.int32, (TILE, 128), 0)
    lane = lax.broadcasted_iota(jnp.int32, (TILE, 128), 1)
    for k in range(NB):
        keep = column <= k
        real = jnp.where(keep, state_real[k], 0.0)
        imag = jnp.where(keep, state_imag[k], 0.0)
        lower = jnp.where(lane == 0, pltpu.roll(real, 96, 1), real)
        joined = jnp.concatenate([real, imag, -imag, lower], axis=0)
        inverse[40 * k : 40 * (k + 1), :] = jnp.transpose(joined)[:40]
    inverse[40 * NB :, :] = jnp.zeros((40, 128), jnp.float32)


def factor_kernel(scale, packed, inverse, state_real, state_imag, tiles):
    factor_lanes(scale, packed, tiles, state_real, state_imag)
    write_inverse(state_real, state_imag, inverse)


STATE = jax.ShapeDtypeStruct((NB, TILE, 128), jnp.float32)
INVERSE = jax.ShapeDtypeStruct((TILE * 40, 128), jnp.float32)


def factor(packed, points_total):
    return pl.pallas_call(
        lambda *refs: factor_kernel(1.0 / points_total, *refs),
        out_shape=(INVERSE, STATE, STATE),
        in_specs=[VMEM],
        out_specs=(VMEM,) * 3,
        scratch_shapes=[pltpu.VMEM(((TILE + 1) * TILE, 128), jnp.float32)],
        compiler_params=pltpu.CompilerParams(vmem_limit_bytes=48 << 20),
        name="factor",
    )(packed.reshape(256, 128))


def finish_kernel(
    scale, packed, first_real, first_imag, inverse, triangle_real, triangle_imag,
    tiles, state_real, state_imag, right_real, right_imag,
):
    factor_lanes(scale, packed, tiles, state_real, state_imag)
    write_inverse(state_real, state_imag, inverse)
    column = lax.broadcasted_iota(jnp.int32, (TILE, 128), 0)
    for k in range(NB):
        real = first_real[k]
        diagonal = jnp.where(column == k, 1.0 / real, 0.0)
        right_real[k] = jnp.where(column > k, real, diagonal)
        right_imag[k] = jnp.where(column > k, first_imag[k], 0.0)
    for i in range(NB):
        own = 1.0 / state_real[i, i : i + 1, :]
        start = (own * right_real[i], own * right_imag[i])

        def gather(k, total):
            total_real, total_imag = total
            pick_real = state_real[i, pl.ds(k, 1), :]
            pick_imag = state_imag[i, pl.ds(k, 1), :]
            row_real = right_real[k]
            row_imag = right_imag[k]
            return (
                total_real + (pick_real * row_real - pick_imag * row_imag),
                total_imag + (pick_real * row_imag + pick_imag * row_real),
            )

        total_real, total_imag = lax.fori_loop(i + 1, NB, gather, start, unroll=True)
        triangle_real[i] = total_real
        triangle_imag[i] = total_imag


def finish(packed, first_real, first_imag, points_total):
    scratch = pltpu.VMEM(STATE.shape, jnp.float32)
    return pl.pallas_call(
        lambda *refs: finish_kernel(1.0 / points_total, *refs),
        out_shape=(INVERSE, STATE, STATE),
        in_specs=[VMEM] * 3,
        out_specs=(VMEM,) * 3,
        scratch_shapes=[pltpu.VMEM(((TILE + 1) * TILE, 128), jnp.float32)] + [scratch] * 4,
        compiler_params=pltpu.CompilerParams(vmem_limit_bytes=48 << 20),
        name="finish",
    )(packed.reshape(256, 128), first_real, first_imag)


def slot_matrix(inverse, slot):
    lines = inverse[pl.ds(slot, TILE, stride=40), :]
    return jnp.concatenate([lines[:, :64], lines[:, 64:]], axis=0)


def first_kernel(spectrum, inverse, ortho, packed):
    for group in range(8):
        tiles = []
        for slot in range(group, SLOTS, 8):
            value = slot_rows(spectrum, slot)
            value = multiply(left6(slot_matrix(inverse, slot)), right6(value))
            ortho[slot] = value
            tiles.append(gram_tile(self_product(value, 2), slot))
        put_tiles(packed, group, tiles)


def first_ortho(spectrum, inverse):
    points = spectrum.shape[0] * 128
    return pl.pallas_call(
        first_kernel,
        out_shape=(
            jax.ShapeDtypeStruct((SLOTS, SEG, points), jnp.float32),
            jax.ShapeDtypeStruct((16, 16, 128), jnp.float32),
        ),
        in_specs=[VMEM] * 2,
        out_specs=(VMEM, VMEM),
        compiler_params=pltpu.CompilerParams(vmem_limit_bytes=48 << 20),
        name="first_ortho",
    )(spectrum, inverse)


def modes_kernel(ortho, inverse, modes, held, sems):
    copies = []
    panels = ortho.shape[2] // 128
    step = 2 * panels

    def put(frequency, part, value):
        for panel in range(panels):
            held[frequency, pl.ds(2 * panel + part, NB, stride=step), :] = value[
                :NB, 128 * panel : 128 * (panel + 1)
            ]

    def send(frequency):
        copy = pltpu.make_async_copy(
            held.at[frequency], modes.at[frequency], sems.at[frequency]
        )
        copy.start()
        copies.append(copy)

    for slot in range(SLOTS):
        value = multiply(left3(slot_matrix(inverse, slot)), right3(ortho[slot]))
        put(slot, 0, value[:TILE])
        if slot:
            put(slot, 1, value[TILE:])
        else:
            nothing = jnp.zeros((TILE, value.shape[1]), jnp.float32)
            put(0, 1, nothing)
            put(NF - 1, 0, value[TILE:])
            put(NF - 1, 1, nothing)
            send(NF - 1)
        send(slot)
    for copy in copies:
        copy.wait()


def final_modes(ortho, inverse):
    points = ortho.shape[2]
    shape = (NF, NB * points // 64, 128)
    modes = pl.pallas_call(
        modes_kernel,
        out_shape=jax.ShapeDtypeStruct(shape, jnp.float32),
        in_specs=[VMEM] * 2,
        out_specs=pl.BlockSpec(memory_space=pl.ANY),
        scratch_shapes=[pltpu.VMEM(shape, jnp.float32), pltpu.SemaphoreType.DMA((NF,))],
        compiler_params=pltpu.CompilerParams(vmem_limit_bytes=48 << 20),
        name="modes",
    )(ortho, inverse)
    modes = modes.reshape(NF, NB, points // 128, 2, 128)
    return jnp.transpose(modes, (3, 0, 1, 2, 4)).reshape(2, NF, NB, points)


def shards(snapshots, weights):
    records = lax.all_to_all(snapshots, "tm", split_axis=1, concat_axis=0, tiled=True)
    points_total = weights.shape[0] * lax.axis_size("tm") * lax.axis_size("pts")
    spectrum, packed = spectra(records, weights)
    inverse, first_real, first_imag = factor(global_sum(packed), points_total)
    ortho, packed = first_ortho(spectrum, inverse)
    inverse, *triangle = finish(global_sum(packed), first_real, first_imag, points_total)
    triangle = jnp.stack([part[:, :NB, :NF] for part in triangle])
    return final_modes(ortho, inverse), jnp.transpose(triangle, (0, 3, 1, 2))


def solution(mesh):
    placed = (P("tm", "pts"), P(("pts", "tm")))
    return jax.shard_map(
        shards,
        mesh=mesh,
        in_specs=placed,
        out_specs=(P(None, None, None, ("pts", "tm")), P()),
        check_vma=False,
    )
```

```python
import jax
import jax.numpy as jnp
import ml_dtypes
import numpy as np
from jax import lax
from jax.experimental import pallas as pl
from jax.experimental.pallas import tpu as pltpu
from jax.sharding import PartitionSpec as P

SEG = 64
HOP = 32
NF = 33
NT = 1024
NB = 31
MESH = pl.DeviceIdType.MESH

VMEM = pl.BlockSpec(memory_space=pltpu.VMEM)
TILE = 32
SLOTS = 32
LINES = SEG + 1
TILE_LINES = TILE + 1
SLOT_LINES = 41


def fourier_table():
    sample = np.arange(SEG)[:, None]
    column = np.arange(SEG)[None, :]
    frequency = np.where(column < NF, column, column - HOP)
    window = 0.5 - 0.5 * np.cos(2.0 * np.pi * sample / SEG)
    phase_angle = 2.0 * np.pi * ((frequency * sample) % SEG) / SEG
    waveform = np.where(column < NF, np.cos(phase_angle), -np.sin(phase_angle))
    return (waveform * window / np.sqrt(3 * SEG / 8)).astype(np.float32)


def table_parts():
    table = fourier_table().T
    high = table.astype(ml_dtypes.bfloat16)
    rest = table - high.astype(np.float32)
    middle = rest.astype(ml_dtypes.bfloat16)
    low = (rest - middle.astype(np.float32)).astype(ml_dtypes.bfloat16)
    return np.concatenate([high, high, middle, high, middle, low], axis=1)


def parts_of(value, count):
    parts = []
    for _ in range(count):
        part = value.astype(jnp.bfloat16)
        parts.append(part)
        value = value - part.astype(jnp.float32)
    return parts


def left6(value):
    high, middle, low = parts_of(value, 3)
    return jnp.concatenate([high, high, middle, high, middle, low], axis=1)


def right6(value):
    high, middle, low = parts_of(value, 3)
    return jnp.concatenate([high, middle, high, low, middle, high], axis=0)


def left3(value):
    high, low = parts_of(value, 2)
    return jnp.concatenate([high, high, low], axis=1)


def right3(value):
    high, low = parts_of(value, 2)
    return jnp.concatenate([high, low, high], axis=0)


def multiply(left, right):
    return jnp.dot(left, right, preferred_element_type=jnp.float32)


def self_product(value, count):
    stacked = jnp.concatenate(parts_of(value, count), axis=0)
    whole = lax.dot_general(
        stacked, stacked, (((1,), (1,)), ((), ())), preferred_element_type=jnp.float32
    )
    size = value.shape[0]
    rows = sum(whole[i * size : (i + 1) * size] for i in reversed(range(count)))
    return sum(rows[:, i * size : (i + 1) * size] for i in reversed(range(count)))


def gram_tile(product, slot):
    top_left = product[:TILE, :TILE]
    bottom_right = product[TILE:, TILE:]
    row = lax.broadcasted_iota(jnp.int32, (TILE, TILE), 0)
    column = lax.broadcasted_iota(jnp.int32, (TILE, TILE), 1)
    if slot == 0:
        return jnp.where(column >= row, top_left, pltpu.roll(bottom_right, 1, 0))
    imaginary = product[:TILE, TILE:] - product[TILE:, :TILE]
    return jnp.where(column >= row, top_left + bottom_right, imaginary)


def put_tiles(out, group, tiles, add):
    joined = jnp.concatenate(tiles, axis=1)
    if add:
        joined = joined + jnp.concatenate([out[2 * group], out[2 * group + 1]], axis=0)
    out[2 * group] = joined[:16]
    out[2 * group + 1] = joined[16:]


def slot_rows(spectrum, slot, panels):
    halves = [
        [
            spectrum[panel, pl.ds(slot + half, TILE, stride=LINES), :]
            for panel in panels
        ]
        for half in (0, 32)
    ]
    return jnp.concatenate([jnp.concatenate(row, axis=1) for row in halves], axis=0)


PIECES = ((0, 384), (384, 128))


def spectrum_kernel(
    snapshots, weights, table, spectrum, result,
    first, second, packed, parts, root, send, recv, own, *sums,
):
    n = lax.axis_size("tm")
    pts = lax.axis_size("pts")
    me = lax.axis_index("tm")
    points = weights.shape[1]
    fetches = [
        pltpu.make_async_copy(table, parts, own.at[2]),
        pltpu.make_async_copy(weights, root, own.at[3]),
    ]
    for fetch in fetches:
        fetch.start()
    each(n, lambda d: greet(ahead("tm", d, n)))
    each(pts, lambda d: greet(ahead("pts", d, pts)))
    pl.semaphore_wait(pltpu.get_barrier_semaphore(), n + pts - 2)
    mine = pl.ds(pl.multiple_of(SEG * me, SEG), SEG)
    pieces = list(zip(range(2), PIECES, (first, second)))

    def column(device, start, width):
        return pl.ds(pl.multiple_of(device * points + start, 128), width)

    def travel(piece, d):
        index, (start, width), target = piece
        to = ahead("tm", d, n)
        return remote(
            snapshots.at[:, column(to["tm"], start, width)],
            target.at[mine, :],
            send.at[index, d],
            recv.at[index, d],
            to,
        )

    def stay(piece):
        index, (start, width), target = piece
        return pltpu.make_async_copy(
            snapshots.at[:, column(me, start, width)], target.at[mine, :], own.at[index]
        )

    for piece in pieces:
        each(n, lambda d: travel(piece, d).start())
        stay(piece).start()
    for fetch in fetches:
        fetch.wait()
    for panel in range(spectrum.shape[0]):
        spectrum[panel, NB * LINES :, :] = jnp.zeros((LINES, 128), jnp.float32)
    for piece in pieces:
        index, (start, width), target = piece
        stay(piece).wait()
        each(n, lambda d: travel(piece, d).wait_recv())
        panels = range(start // 128, (start + width) // 128)
        scale = jnp.sqrt(root[:, start : start + width])

        for b in range(NB):
            rows = target[HOP * b : HOP * b + SEG, :]
            value = multiply(parts[...], right6(rows)) * scale
            for panel in panels:
                at = 128 * panel - start
                spectrum[panel, LINES * b : LINES * b + SEG, :] = value[:, at : at + 128]
        for group in range(8):
            tiles = []
            for slot in range(group, SLOTS, 8):
                value = slot_rows(spectrum, slot, panels)
                tiles.append(gram_tile(self_product(value, 3), slot))
            put_tiles(packed, group, tiles, index > 0)
    for piece in pieces:
        each(n, lambda d: travel(piece, d).wait_send())
    sum_stages(packed, result, *sums)


def spectra(snapshots, weights):
    points = weights.shape[0]
    n = lax.axis_size("tm")
    dma = pltpu.SemaphoreType.DMA
    return pl.pallas_call(
        spectrum_kernel,
        out_shape=(
            jax.ShapeDtypeStruct((points // 128, TILE * LINES, 128), jnp.float32),
            jax.ShapeDtypeStruct(CHUNKS, jnp.float32),
        ),
        in_specs=[pl.BlockSpec(memory_space=pltpu.HBM)] * 3,
        out_specs=(VMEM, VMEM),
        scratch_shapes=[pltpu.VMEM((NT, width), jnp.float32) for _, width in PIECES]
        + [
            pltpu.VMEM(CHUNKS, jnp.float32),
            pltpu.VMEM((SEG, 6 * SEG), jnp.bfloat16),
            pltpu.VMEM((1, points), jnp.float32),
            dma((2, n)),
            dma((2, n)),
            dma((4,)),
        ]
        + sum_scratch(),
        compiler_params=pltpu.CompilerParams(
            vmem_limit_bytes=24 << 20, collective_id=0, has_side_effects=True
        ),
        name="spectra",
    )(*(pltpu.with_memory_space_constraint(x, pltpu.HBM) for x in (snapshots, weights.reshape(1, points), jnp.asarray(table_parts()))))


def remote(source, target, send, recv, device):
    return pltpu.make_async_remote_copy(
        src_ref=source, dst_ref=target, send_sem=send, recv_sem=recv,
        device_id=device, device_id_type=MESH,
    )


def each(count, action):
    def step(d, carry):
        action(d)
        return carry

    lax.fori_loop(1, count, step, 0)


def greet(device):
    pl.semaphore_signal(
        pltpu.get_barrier_semaphore(), inc=1, device_id=device, device_id_type=MESH
    )


def ahead(axis, d, n):
    return {axis: lax.rem(lax.axis_index(axis) + d, n)}


def sibling():
    me = lax.axis_index("tm")
    return {"tm": me + 1 - 2 * lax.rem(me, 2)}


def sum_stages(x_ref, o_ref, half, part, total, share, whole, full, *sems):
    send0, recv0, send1, recv1, send2, recv2, send3, recv3, send4, recv4 = sems
    me_p = lax.axis_index("pts")
    me_t = lax.axis_index("tm")
    core = lax.rem(me_t, 2)
    chip = me_t // 2
    n = part.shape[0]
    chips = share.shape[0]
    own_lines = pl.ds(pl.multiple_of(8 * core, 8), 8)
    other_lines = pl.ds(pl.multiple_of(8 - 8 * core, 8), 8)
    swap = remote(x_ref.at[:, other_lines, :], half, send0, recv0, sibling())

    def scatter(d):
        to = ahead("pts", d, n)
        return remote(full.at[to["pts"]], part.at[d], send1.at[d], recv1.at[d], to)

    def exchange(d):
        to = ahead("tm", 2 * d, 2 * chips)
        return remote(total, share.at[chip], send2.at[d], recv2.at[d], to)

    def gather(d):
        to = ahead("pts", d, n)
        return remote(whole, o_ref.at[me_p, own_lines, :], send3.at[d], recv3.at[d], to)

    back = remote(
        o_ref.at[:, own_lines, :], o_ref.at[:, own_lines, :], send4, recv4, sibling()
    )
    swap.start()
    swap.wait_recv()
    full[...] = x_ref[:, own_lines, :] + half[...]
    each(n, lambda d: scatter(d).start())
    part[0] = full[me_p]
    each(n, lambda d: scatter(d).wait_recv())
    total[...] = jnp.sum(part[...], axis=0)
    each(chips, lambda d: exchange(d).start())
    share[chip] = total[...]
    each(chips, lambda d: exchange(d).wait_recv())
    whole[...] = jnp.sum(share[...], axis=0)
    each(n, lambda d: gather(d).start())
    o_ref[me_p, own_lines, :] = whole[...]
    each(n, lambda d: gather(d).wait_recv())
    back.start()
    swap.wait_send()
    each(n, lambda d: scatter(d).wait_send())
    each(chips, lambda d: exchange(d).wait_send())
    each(n, lambda d: gather(d).wait_send())
    back.wait()


CHUNKS = (16, 16, 128)


def sum_scratch():
    n, lines, lanes = CHUNKS
    chips = lax.axis_size("tm") // 2
    dma = pltpu.SemaphoreType.DMA
    buffer = pltpu.VMEM((n, lines // 2, lanes), jnp.float32)
    return [
        buffer,
        buffer,
        pltpu.VMEM((lines // 2, lanes), jnp.float32),
        pltpu.VMEM((chips, lines // 2, lanes), jnp.float32),
        pltpu.VMEM((lines // 2, lanes), jnp.float32),
        buffer,
        dma, dma, dma((n,)), dma((n,)), dma((chips,)), dma((chips,)),
        dma((n,)), dma((n,)), dma, dma,
    ]


def factor_lanes(scale, packed, tiles, state_real, state_imag):
    column = lax.broadcasted_iota(jnp.int32, (TILE, 128), 0)
    lane = lax.broadcasted_iota(jnp.int32, (TILE, 128), 1)
    for b in range(TILE):
        lines = packed[pl.ds(b, 8, stride=TILE), :]
        spread = jnp.concatenate(
            [lines] + [pltpu.roll(lines, 128 - 32 * s, 1) for s in (1, 2, 3)]
            + [jnp.zeros((96, 128), jnp.float32)],
            axis=0,
        )
        line = TILE_LINES * b
        tiles[line : line + TILE, :] = jnp.transpose(spread)[:TILE] * scale
    tiles[TILE * TILE_LINES :, :] = jnp.zeros((TILE, 128), jnp.float32)
    for b in range(NB):
        line = TILE_LINES * b
        straight = tiles[line : line + TILE, :]
        turned = tiles[pl.ds(b, TILE, stride=TILE_LINES), :]
        line = TILE_LINES * (b + 1)
        below = tiles[line : line + TILE, :]
        below_turned = tiles[pl.ds(TILE_LINES + b, TILE, stride=TILE_LINES), :]
        last = pltpu.roll(jnp.where(column <= b, below, below_turned), 32, 1)
        real = jnp.where(column >= b, straight, turned)
        real = jnp.where(lane == 32, last, real)
        imag = jnp.where(column < b, straight, -turned)
        state_real[b] = jnp.where(lane > 32, jnp.where(column == b, 1.0, 0.0), real)
        state_imag[b] = jnp.where(
            (lane == 0) | (lane >= 32) | (column == b), 0.0, imag
        )
    for k in range(NB):
        here = column == k
        inverse = 1.0 / jnp.sqrt(state_real[k, k : k + 1, :])
        row_real = jnp.where(here, inverse, state_real[k] * inverse)
        row_imag = jnp.where(here, 0.0, state_imag[k] * inverse)
        state_real[k] = row_real
        state_imag[k] = row_imag

        def eliminate(i, carry):
            pick_real = state_real[k, pl.ds(i, 1), :]
            pick_imag = state_imag[k, pl.ds(i, 1), :]
            work_real = jnp.where(here, 0.0, state_real[i])
            work_imag = jnp.where(here, 0.0, state_imag[i])
            state_real[i] = work_real - (pick_real * row_real + pick_imag * row_imag)
            state_imag[i] = work_imag - (pick_real * row_imag - pick_imag * row_real)
            return carry

        lax.fori_loop(k + 1, NB, eliminate, 0, unroll=True)


def write_inverse(state_real, state_imag, inverse):
    column = lax.broadcasted_iota(jnp.int32, (TILE, 128), 0)
    lane = lax.broadcasted_iota(jnp.int32, (TILE, 128), 1)
    for k in range(NB):
        keep = column <= k
        real = jnp.where(keep, state_real[k], 0.0)
        imag = jnp.where(keep, state_imag[k], 0.0)
        lower = jnp.where(lane == 0, pltpu.roll(real, 96, 1), real)
        joined = jnp.concatenate([real, imag, -imag, lower], axis=0)
        line = SLOT_LINES * k
        inverse[line : line + SLOTS, :] = jnp.transpose(joined)[:SLOTS]
    line = SLOT_LINES * NB
    inverse[line : line + SLOTS, :] = jnp.zeros((SLOTS, 128), jnp.float32)


def factor_kernel(scale, packed, inverse, state_real, state_imag, tiles):
    factor_lanes(scale, packed, tiles, state_real, state_imag)
    write_inverse(state_real, state_imag, inverse)


TILES = pltpu.VMEM((TILE * TILE_LINES + TILE, 128), jnp.float32)
STATE = jax.ShapeDtypeStruct((NB, TILE, 128), jnp.float32)
INVERSE = jax.ShapeDtypeStruct((TILE * SLOT_LINES, 128), jnp.float32)


def factor(packed, points_total):
    return pl.pallas_call(
        lambda *refs: factor_kernel(1.0 / points_total, *refs),
        out_shape=(INVERSE, STATE, STATE),
        in_specs=[VMEM],
        out_specs=(VMEM,) * 3,
        scratch_shapes=[TILES],
        compiler_params=pltpu.CompilerParams(vmem_limit_bytes=24 << 20),
        name="factor",
    )(packed.reshape(256, 128))


def slot_matrix(inverse, slot):
    lines = inverse[pl.ds(slot, TILE, stride=SLOT_LINES), :]
    return jnp.concatenate([lines[:, :64], lines[:, 64:]], axis=0)


def first_kernel(spectrum, inverse, ortho, result, packed, *sums):
    pts = lax.axis_size("pts")
    chips = lax.axis_size("tm") // 2
    greet(sibling())
    each(pts, lambda d: greet(ahead("pts", d, pts)))
    each(chips, lambda d: greet(ahead("tm", 2 * d, 2 * chips)))
    for slot in range(SLOTS):
        value = slot_rows(spectrum, slot, range(spectrum.shape[0]))
        ortho[slot] = multiply(left6(slot_matrix(inverse, slot)), right6(value))
    for group in range(8):
        tiles = [
            gram_tile(self_product(ortho[slot], 2), slot)
            for slot in range(group, SLOTS, 8)
        ]
        put_tiles(packed, group, tiles, False)
    pl.semaphore_wait(pltpu.get_barrier_semaphore(), pts + chips - 1)
    sum_stages(packed, result, *sums)


def first_ortho(spectrum, inverse):
    points = spectrum.shape[0] * 128
    return pl.pallas_call(
        first_kernel,
        out_shape=(
            jax.ShapeDtypeStruct((SLOTS, SEG, points), jnp.float32),
            jax.ShapeDtypeStruct(CHUNKS, jnp.float32),
        ),
        in_specs=[VMEM] * 2,
        out_specs=(VMEM, VMEM),
        scratch_shapes=[pltpu.VMEM(CHUNKS, jnp.float32)] + sum_scratch(),
        compiler_params=pltpu.CompilerParams(
            vmem_limit_bytes=24 << 20, collective_id=1, has_side_effects=True
        ),
        name="first_ortho",
    )(spectrum, inverse)


def send_modes(ortho, inverse, modes, held, sems):
    copies = []
    panels = ortho.shape[2] // 128
    step = 2 * panels

    def put(frequency, part, value):
        for panel in range(panels):
            held[frequency, pl.ds(2 * panel + part, NB, stride=step), :] = value[
                :NB, 128 * panel : 128 * (panel + 1)
            ]

    def send(frequency):
        copy = pltpu.make_async_copy(
            held.at[frequency], modes.at[frequency], sems.at[frequency]
        )
        copy.start()
        copies.append(copy)

    for slot in range(SLOTS):
        value = multiply(left3(slot_matrix(inverse, slot)), right3(ortho[slot]))
        put(slot, 0, value[:TILE])
        if slot:
            put(slot, 1, value[TILE:])
        else:
            nothing = jnp.zeros((TILE, value.shape[1]), jnp.float32)
            put(0, 1, nothing)
            put(NF - 1, 0, value[TILE:])
            put(NF - 1, 1, nothing)
            send(NF - 1)
        send(slot)
    return copies


def finish_kernel(
    scale, packed, ortho, first_real, first_imag, modes, triangle,
    held, sems, inverse, tiles, state_real, state_imag, right_real, right_imag,
):
    factor_lanes(scale, packed, tiles, state_real, state_imag)
    write_inverse(state_real, state_imag, inverse)
    copies = send_modes(ortho, inverse, modes, held, sems)
    column = lax.broadcasted_iota(jnp.int32, (TILE, 128), 0)
    for k in range(NB):
        real = first_real[k]
        diagonal = jnp.where(column == k, 1.0 / real, 0.0)
        right_real[k] = jnp.where(column > k, real, diagonal)
        right_imag[k] = jnp.where(column > k, first_imag[k], 0.0)
    for i in range(NB):
        own = 1.0 / state_real[i, i : i + 1, :]
        start = (own * right_real[i], own * right_imag[i])

        def gather(k, total):
            total_real, total_imag = total
            pick_real = state_real[i, pl.ds(k, 1), :]
            pick_imag = state_imag[i, pl.ds(k, 1), :]
            row_real = right_real[k]
            row_imag = right_imag[k]
            return (
                total_real + (pick_real * row_real - pick_imag * row_imag),
                total_imag + (pick_real * row_imag + pick_imag * row_real),
            )

        total = lax.fori_loop(i + 1, NB, gather, start, unroll=True)
        for part in range(2):
            triangle[i, pl.ds(part, NB, stride=2), :] = total[part][:NB]
    for copy in copies:
        copy.wait()


def finish(packed, ortho, first_real, first_imag, points_total):
    points = ortho.shape[2]
    shape = (NF, NB * points // 64, 128)
    modes, triangle = pl.pallas_call(
        lambda *refs: finish_kernel(1.0 / points_total, *refs),
        out_shape=(
            jax.ShapeDtypeStruct(shape, jnp.float32),
            jax.ShapeDtypeStruct((NB, 2 * NB, 128), jnp.float32),
        ),
        in_specs=[VMEM] * 4,
        out_specs=(pl.BlockSpec(memory_space=pl.ANY), VMEM),
        scratch_shapes=[
            pltpu.VMEM(shape, jnp.float32),
            pltpu.SemaphoreType.DMA((NF,)),
            pltpu.VMEM(INVERSE.shape, jnp.float32),
            TILES,
        ]
        + [pltpu.VMEM(STATE.shape, jnp.float32)] * 4,
        compiler_params=pltpu.CompilerParams(vmem_limit_bytes=24 << 20),
        name="finish",
    )(packed.reshape(256, 128), ortho, first_real, first_imag)
    modes = modes.reshape(NF, NB, points // 128, 2, 128)
    modes = jnp.transpose(modes, (3, 0, 1, 2, 4)).reshape(2, NF, NB, points)
    triangle = triangle.reshape(NB, NB, 2, 128)[..., :NF]
    return modes, jnp.transpose(triangle, (2, 3, 0, 1))


def shards(snapshots, weights):
    points_total = weights.shape[0] * lax.axis_size("tm") * lax.axis_size("pts")
    spectrum, packed = spectra(snapshots, weights)
    inverse, first_real, first_imag = factor(packed, points_total)
    ortho, packed = first_ortho(spectrum, inverse)
    return finish(packed, ortho, first_real, first_imag, points_total)


def solution(mesh):
    placed = (P("tm", "pts"), P(("pts", "tm")))
    return jax.shard_map(
        shards,
        mesh=mesh,
        in_specs=placed,
        out_specs=(P(None, None, None, ("pts", "tm")), P()),
        check_vma=False,
    )
```

```python
import math

import jax
import jax.numpy as jnp
import ml_dtypes
import numpy as np
from jax import lax
from jax.experimental import pallas as pl
from jax.experimental.pallas import tpu as pltpu
from jax.sharding import PartitionSpec as P

SEG = 64
HOP = 32
NF = 33
NT = 1024
NB = 31
MESH = pl.DeviceIdType.MESH

VMEM = pl.BlockSpec(memory_space=pltpu.VMEM)
TILE = 32
SLOTS = 32
LINES = SEG + 1
TILE_LINES = TILE + 1
SLOT_LINES = 41


def fourier_table():
    sample = np.arange(SEG)[:, None]
    column = np.arange(SEG)[None, :]
    frequency = np.where(column < NF, column, column - HOP)
    window = 0.5 - 0.5 * np.cos(2.0 * np.pi * sample / SEG)
    phase_angle = 2.0 * np.pi * ((frequency * sample) % SEG) / SEG
    waveform = np.where(column < NF, np.cos(phase_angle), -np.sin(phase_angle))
    return (waveform * window / np.sqrt(3 * SEG / 8)).astype(np.float32)


def table_parts():
    table = fourier_table().T
    high = table.astype(ml_dtypes.bfloat16)
    rest = table - high.astype(np.float32)
    middle = rest.astype(ml_dtypes.bfloat16)
    low = (rest - middle.astype(np.float32)).astype(ml_dtypes.bfloat16)
    return np.concatenate([high, high, middle, high, middle, low], axis=1)


def parts_of(value, count):
    parts = []
    for _ in range(count):
        part = value.astype(jnp.bfloat16)
        parts.append(part)
        value = value - part.astype(jnp.float32)
    return parts


def left6(value):
    high, middle, low = parts_of(value, 3)
    return jnp.concatenate([high, high, middle, high, middle, low], axis=1)


def right6(value):
    high, middle, low = parts_of(value, 3)
    return jnp.concatenate([high, middle, high, low, middle, high], axis=0)


def left3(value):
    high, low = parts_of(value, 2)
    return jnp.concatenate([high, high, low], axis=1)


def right3(value):
    high, low = parts_of(value, 2)
    return jnp.concatenate([high, low, high], axis=0)


def multiply(left, right):
    return jnp.dot(left, right, preferred_element_type=jnp.float32)


def self_product(value, count):
    stacked = jnp.concatenate(parts_of(value, count), axis=0)
    whole = lax.dot_general(
        stacked, stacked, (((1,), (1,)), ((), ())), preferred_element_type=jnp.float32
    )
    size = value.shape[0]
    rows = sum(whole[i * size : (i + 1) * size] for i in reversed(range(count)))
    return sum(rows[:, i * size : (i + 1) * size] for i in reversed(range(count)))


def gram_tile(product, slot):
    top_left = product[:TILE, :TILE]
    bottom_right = product[TILE:, TILE:]
    row = lax.broadcasted_iota(jnp.int32, (TILE, TILE), 0)
    column = lax.broadcasted_iota(jnp.int32, (TILE, TILE), 1)
    if slot == 0:
        return jnp.where(column >= row, top_left, pltpu.roll(bottom_right, 1, 0))
    imaginary = product[:TILE, TILE:] - product[TILE:, :TILE]
    return jnp.where(column >= row, top_left + bottom_right, imaginary)


def put_tiles(out, group, tiles, add):
    joined = jnp.concatenate(tiles, axis=1)
    if add:
        joined = joined + jnp.concatenate([out[2 * group], out[2 * group + 1]], axis=0)
    out[2 * group] = joined[:16]
    out[2 * group + 1] = joined[16:]


def slot_rows(spectrum, slot, panels):
    halves = [
        [
            spectrum[panel, pl.ds(slot + half, TILE, stride=LINES), :]
            for panel in panels
        ]
        for half in (0, 32)
    ]
    return jnp.concatenate([jnp.concatenate(row, axis=1) for row in halves], axis=0)


def remote(source, target, send, recv, device):
    return pltpu.make_async_remote_copy(
        src_ref=source, dst_ref=target, send_sem=send, recv_sem=recv,
        device_id=device, device_id_type=MESH,
    )


def greet(device):
    pl.semaphore_signal(
        pltpu.get_barrier_semaphore(), inc=1, device_id=device, device_id_type=MESH
    )


def ring_offsets(n):
    return sorted(range(1, n), key=lambda d: -min(d, n - d))


def square_offsets(n):
    side = math.isqrt(n)
    offsets = [(i, j) for i in range(side) for j in range(side) if i or j]
    return sorted(
        offsets, key=lambda o: -(min(o[0], side - o[0]) + min(o[1], side - o[1]))
    )


def sum_stages(x_ref, o_ref, part, total, share, whole, *sems):
    send1, recv1, send2, recv2, send3, recv3 = sems
    me_p = lax.axis_index("pts")
    me_t = lax.axis_index("tm")
    core = lax.rem(me_t, 2)
    chip = me_t // 2
    n = part.shape[0] // 2
    side = math.isqrt(n)
    chips = share.shape[0]

    def lines(k):
        return pl.ds(pl.multiple_of(8 * k, 8), 8)

    own_lines = pl.ds(pl.multiple_of(16 * me_p + 8 * core, 8), 8)
    peers = [(i, j, c) for i, j in square_offsets(n) for c in (0, 1)] + [(0, 0, 1)]

    def peer(offset):
        i, j, c = offset
        row = lax.rem(me_p // side + i, side)
        to_p = row * side + lax.rem(lax.rem(me_p, side) + j, side)
        to_core = lax.rem(core + c, 2)
        device = {"pts": to_p, "tm": me_t - core + to_core}
        return device, to_p, to_core, (i * side + j) * 2 + c

    def scatter(offset):
        device, to_p, to_core, slot = peer(offset)
        return remote(
            x_ref.at[to_p, lines(to_core), :], part.at[slot],
            send1.at[slot], recv1.at[slot], device,
        )

    def exchange(d):
        to = {"tm": lax.rem(me_t + 2 * d, 2 * chips)}
        return remote(total, share.at[chip], send2.at[d], recv2.at[d], to)

    def gather(offset):
        device, _, _, slot = peer(offset)
        return remote(
            whole, o_ref.at[own_lines, :], send3.at[slot], recv3.at[slot], device
        )

    scatters = [scatter(offset) for offset in peers]
    exchanges = [exchange(d) for d in ring_offsets(chips)]
    gathers = [gather(offset) for offset in peers]
    for copy in scatters:
        copy.start()
    part[0] = x_ref[me_p, lines(core), :]
    for copy in scatters:
        copy.wait_recv()
    total[...] = jnp.sum(part[...], axis=0)
    for copy in exchanges:
        copy.start()
    share[chip] = total[...]
    for copy in exchanges:
        copy.wait_recv()
    whole[...] = jnp.sum(share[...], axis=0)
    for copy in gathers:
        copy.start()
    o_ref[own_lines, :] = whole[...]
    for copy in gathers:
        copy.wait_recv()
    for copy in scatters + exchanges + gathers:
        copy.wait_send()


def all_greetings():
    n = lax.axis_size("pts")
    side = math.isqrt(n)
    me_p = lax.axis_index("pts")
    me_t = lax.axis_index("tm")
    core = lax.rem(me_t, 2)
    chips = lax.axis_size("tm") // 2
    devices = [{"tm": lax.rem(me_t + 2 * d, 2 * chips)} for d in ring_offsets(chips)]
    for i, j in square_offsets(n):
        row = lax.rem(me_p // side + i, side)
        to_p = row * side + lax.rem(lax.rem(me_p, side) + j, side)
        devices.append({"pts": to_p})
        devices.append({"pts": to_p, "tm": me_t + 1 - 2 * core})
    devices.append({"tm": me_t + 1 - 2 * core})
    return devices


CHUNKS = (16, 16, 128)
SUMS = (256, 128)


def sum_scratch():
    n, lines, lanes = CHUNKS
    chips = lax.axis_size("tm") // 2
    dma = pltpu.SemaphoreType.DMA
    piece = (lines // 2, lanes)
    return [
        pltpu.VMEM((2 * n,) + piece, jnp.float32),
        pltpu.VMEM(piece, jnp.float32),
        pltpu.VMEM((chips,) + piece, jnp.float32),
        pltpu.VMEM(piece, jnp.float32),
        dma((2 * n,)), dma((2 * n,)), dma((chips,)), dma((chips,)),
        dma((2 * n,)), dma((2 * n,)),
    ]


def factor_lanes(scale, packed, tiles, state_real, state_imag):
    column = lax.broadcasted_iota(jnp.int32, (TILE, 128), 0)
    lane = lax.broadcasted_iota(jnp.int32, (TILE, 128), 1)
    for b in range(TILE):
        lines = packed[pl.ds(b, 8, stride=TILE), :]
        spread = jnp.concatenate(
            [lines] + [pltpu.roll(lines, 128 - 32 * s, 1) for s in (1, 2, 3)]
            + [jnp.zeros((96, 128), jnp.float32)],
            axis=0,
        )
        line = TILE_LINES * b
        tiles[line : line + TILE, :] = jnp.transpose(spread)[:TILE] * scale
    tiles[TILE * TILE_LINES :, :] = jnp.zeros((TILE, 128), jnp.float32)
    for b in range(NB):
        line = TILE_LINES * b
        straight = tiles[line : line + TILE, :]
        turned = tiles[pl.ds(b, TILE, stride=TILE_LINES), :]
        line = TILE_LINES * (b + 1)
        below = tiles[line : line + TILE, :]
        below_turned = tiles[pl.ds(TILE_LINES + b, TILE, stride=TILE_LINES), :]
        last = pltpu.roll(jnp.where(column <= b, below, below_turned), 32, 1)
        real = jnp.where(column >= b, straight, turned)
        real = jnp.where(lane == 32, last, real)
        imag = jnp.where(column < b, straight, -turned)
        state_real[b] = jnp.where(lane > 32, jnp.where(column == b, 1.0, 0.0), real)
        state_imag[b] = jnp.where(
            (lane == 0) | (lane >= 32) | (column == b), 0.0, imag
        )
    line = lax.broadcasted_iota(jnp.int32, (8, 128), 0)
    for k in range(NB):
        here = line == k % 8
        pivot = state_real[k, k : k + 1, :]
        inverse = lax.rsqrt(pivot)
        inverse = inverse * (1.5 - (0.5 * pivot * inverse) * inverse)
        rows = []
        for at in range(0, TILE, 8):
            group = slice(at, at + 8)
            real = state_real[k, group] * inverse
            imag = state_imag[k, group] * inverse
            if at == k // 8 * 8:
                real = jnp.where(here, inverse, real)
                imag = jnp.where(here, 0.0, imag)
            state_real[k, group] = real
            state_imag[k, group] = imag
            rows.append((real, imag))
        for i in range(k + 1, NB):
            pick_real = state_real[k, i : i + 1]
            pick_imag = state_imag[k, i : i + 1]
            for at in range(0, TILE, 8):
                if at > k and at + 7 < i:
                    continue
                group = slice(at, at + 8)
                real, imag = rows[at // 8]
                work_real = state_real[i, group]
                work_imag = state_imag[i, group]
                if at == k // 8 * 8:
                    work_real = jnp.where(here, 0.0, work_real)
                    work_imag = jnp.where(here, 0.0, work_imag)
                state_real[i, group] = work_real - (pick_real * real + pick_imag * imag)
                state_imag[i, group] = work_imag - (pick_real * imag - pick_imag * real)


def write_inverse(state_real, state_imag, inverse):
    column = lax.broadcasted_iota(jnp.int32, (TILE, 128), 0)
    lane = lax.broadcasted_iota(jnp.int32, (TILE, 128), 1)
    for k in range(NB):
        keep = column <= k
        real = jnp.where(keep, state_real[k], 0.0)
        imag = jnp.where(keep, state_imag[k], 0.0)
        lower = jnp.where(lane == 0, pltpu.roll(real, 96, 1), real)
        joined = jnp.concatenate([real, imag, -imag, lower], axis=0)
        line = SLOT_LINES * k
        inverse[line : line + SLOTS, :] = jnp.transpose(joined)[:SLOTS]
    line = SLOT_LINES * NB
    inverse[line : line + SLOTS, :] = jnp.zeros((SLOTS, 128), jnp.float32)


TILES = pltpu.VMEM((TILE * TILE_LINES + TILE, 128), jnp.float32)
STATE = jax.ShapeDtypeStruct((NB, TILE, 128), jnp.float32)
INVERSE = (TILE * SLOT_LINES, 128)


def slot_matrix(inverse, slot):
    lines = inverse[pl.ds(slot, TILE, stride=SLOT_LINES), :]
    return jnp.concatenate([lines[:, :64], lines[:, 64:]], axis=0)


PIECES = ((0, 384), (384, 128))


def first_kernel(
    points_total, snapshots, weights, table, ortho, result, state_real, state_imag,
    first, second, packed, parts, root, send, recv, own, spectrum, inverse, tiles, gathered,
    *sums,
):
    n = lax.axis_size("tm")
    me = lax.axis_index("tm")
    points = weights.shape[1]
    fetches = [
        pltpu.make_async_copy(table, parts, own.at[2]),
        pltpu.make_async_copy(weights, root, own.at[3]),
    ]
    for fetch in fetches:
        fetch.start()
    chips = n // 2
    core = lax.rem(me, 2)
    others = [(d, c) for d in ring_offsets(chips) for c in (0, 1)] + [(0, 1)]

    def other(offset):
        d, c = offset
        to = lax.rem(me - core + 2 * d, n) + lax.rem(core + c, 2)
        return to, 2 * d + c

    for d in ring_offsets(chips):
        greet({"tm": other((d, 1))[0]})
    devices = all_greetings()
    for device in devices:
        greet(device)
    greeted = len(devices) + chips - 1
    pl.semaphore_wait(pltpu.get_barrier_semaphore(), greeted)
    mine = pl.ds(pl.multiple_of(SEG * me, SEG), SEG)
    pieces = list(zip(range(2), PIECES, (first, second)))

    def column(device, start, width):
        return pl.ds(pl.multiple_of(device * points + start, 128), width)

    def travel(piece, offset):
        index, (start, width), target = piece
        to, slot = other(offset)
        return remote(
            snapshots.at[:, column(to, start, width)],
            target.at[mine, :],
            send.at[index, slot],
            recv.at[index, slot],
            {"tm": to},
        )

    def stay(piece):
        index, (start, width), target = piece
        return pltpu.make_async_copy(
            snapshots.at[:, column(me, start, width)], target.at[mine, :], own.at[index]
        )

    for piece in pieces:
        for offset in others:
            travel(piece, offset).start()
        stay(piece).start()
    for fetch in fetches:
        fetch.wait()
    for panel in range(spectrum.shape[0]):
        spectrum[panel, NB * LINES :, :] = jnp.zeros((LINES, 128), jnp.float32)
    for piece in pieces:
        index, (start, width), target = piece
        stay(piece).wait()
        for offset in others:
            travel(piece, offset).wait_recv()
        panels = range(start // 128, (start + width) // 128)
        scale = jnp.sqrt(root[:, start : start + width])

        for b in range(NB):
            rows = target[HOP * b : HOP * b + SEG, :]
            value = multiply(parts[...], right6(rows)) * scale
            for panel in panels:
                at = 128 * panel - start
                spectrum[panel, LINES * b : LINES * b + SEG, :] = value[:, at : at + 128]
        for group in range(8):
            products = [
                gram_tile(self_product(slot_rows(spectrum, slot, panels), 3), slot)
                for slot in range(group, SLOTS, 8)
            ]
            put_tiles(packed, group, products, index > 0)
    half = len(sums) // 2
    sum_stages(packed, gathered, *sums[:half])
    factor_lanes(1.0 / points_total, gathered, tiles, state_real, state_imag)
    write_inverse(state_real, state_imag, inverse)
    for slot in range(SLOTS):
        value = slot_rows(spectrum, slot, range(spectrum.shape[0]))
        ortho[slot] = multiply(left6(slot_matrix(inverse, slot)), right6(value))
    for group in range(8):
        products = [
            gram_tile(self_product(ortho[slot], 2), slot)
            for slot in range(group, SLOTS, 8)
        ]
        put_tiles(packed, group, products, False)
    sum_stages(packed, result, *sums[half:])
    for piece in pieces:
        for offset in others:
            travel(piece, offset).wait_send()


def first_pass(snapshots, weights, points_total):
    points = weights.shape[0]
    n = lax.axis_size("tm")
    dma = pltpu.SemaphoreType.DMA
    inputs = (snapshots, weights.reshape(1, points), jnp.asarray(table_parts()))
    return pl.pallas_call(
        lambda *refs: first_kernel(points_total, *refs),
        out_shape=(
            jax.ShapeDtypeStruct((SLOTS, SEG, points), jnp.float32),
            jax.ShapeDtypeStruct(SUMS, jnp.float32),
            STATE,
            STATE,
        ),
        in_specs=[pl.BlockSpec(memory_space=pltpu.HBM)] * 3,
        out_specs=(VMEM,) * 4,
        scratch_shapes=[pltpu.VMEM((NT, width), jnp.float32) for _, width in PIECES]
        + [
            pltpu.VMEM(CHUNKS, jnp.float32),
            pltpu.VMEM((SEG, 6 * SEG), jnp.bfloat16),
            pltpu.VMEM((1, points), jnp.float32),
            dma((2, n)),
            dma((2, n)),
            dma((4,)),
            pltpu.VMEM((points // 128, TILE * LINES, 128), jnp.float32),
            pltpu.VMEM(INVERSE, jnp.float32),
            TILES,
            pltpu.VMEM(SUMS, jnp.float32),
        ]
        + sum_scratch() * 2,
        compiler_params=pltpu.CompilerParams(
            vmem_limit_bytes=32 << 20, collective_id=0, has_side_effects=True
        ),
        name="first_pass",
    )(*(pltpu.with_memory_space_constraint(x, pltpu.HBM) for x in inputs))


def send_modes(ortho, inverse, modes, held, sems):
    copies = []
    panels = ortho.shape[2] // 128
    step = 2 * panels

    def put(frequency, part, value):
        for panel in range(panels):
            held[frequency, pl.ds(2 * panel + part, NB, stride=step), :] = value[
                :NB, 128 * panel : 128 * (panel + 1)
            ]

    def send(frequency):
        copy = pltpu.make_async_copy(
            held.at[frequency], modes.at[frequency], sems.at[frequency]
        )
        copy.start()
        copies.append(copy)

    for slot in range(SLOTS):
        value = multiply(left3(slot_matrix(inverse, slot)), right3(ortho[slot]))
        put(slot, 0, value[:TILE])
        if slot:
            put(slot, 1, value[TILE:])
        else:
            nothing = jnp.zeros((TILE, value.shape[1]), jnp.float32)
            put(0, 1, nothing)
            put(NF - 1, 0, value[TILE:])
            put(NF - 1, 1, nothing)
            send(NF - 1)
        send(slot)
    return copies


def finish_kernel(
    scale, packed, ortho, first_real, first_imag, modes, triangle,
    held, sems, inverse, tiles, state_real, state_imag, right_real, right_imag, rows, row_sems,
):
    factor_lanes(scale, packed, tiles, state_real, state_imag)
    write_inverse(state_real, state_imag, inverse)
    copies = send_modes(ortho, inverse, modes, held, sems)
    column = lax.broadcasted_iota(jnp.int32, (TILE, 128), 0)
    for k in range(NB):
        real = first_real[k]
        diagonal = jnp.where(column == k, 1.0 / real, 0.0)
        right_real[k] = jnp.where(column > k, real, diagonal)
        right_imag[k] = jnp.where(column > k, first_imag[k], 0.0)
    for i in range(NB):
        first = i // 8 * 8
        own = 1.0 / state_real[i, i : i + 1, :]
        groups = range(first, TILE, 8)
        total_real = {at: own * right_real[i, at : at + 8] for at in groups}
        total_imag = {at: own * right_imag[i, at : at + 8] for at in groups}
        for k in range(i + 1, NB):
            pick_real = state_real[i, k : k + 1]
            pick_imag = state_imag[i, k : k + 1]
            for at in range(k // 8 * 8, TILE, 8):
                real = right_real[k, at : at + 8]
                imag = right_imag[k, at : at + 8]
                total_real[at] = total_real[at] + (pick_real * real - pick_imag * imag)
                total_imag[at] = total_imag[at] + (pick_real * imag + pick_imag * real)
        for part, total in enumerate((total_real, total_imag)):
            zeros = [jnp.zeros((8, 128), jnp.float32)] * (first // 8)
            line = jnp.concatenate(zeros + [total[at] for at in groups], axis=0)
            rows[i, :, part, :] = line[:NB, :NF]
        copy = pltpu.make_async_copy(rows.at[i], triangle.at[i], row_sems.at[i])
        copy.start()
        copies.append(copy)
    for copy in copies:
        copy.wait()


def finish(packed, ortho, first_real, first_imag, points_total):
    points = ortho.shape[2]
    shape = (NF, NB * points // 64, 128)
    modes, triangle = pl.pallas_call(
        lambda *refs: finish_kernel(1.0 / points_total, *refs),
        out_shape=(
            jax.ShapeDtypeStruct(shape, jnp.float32),
            jax.ShapeDtypeStruct((NB, NB, 2, NF), jnp.float32),
        ),
        in_specs=[VMEM] * 4,
        out_specs=(pl.BlockSpec(memory_space=pl.ANY),) * 2,
        scratch_shapes=[
            pltpu.VMEM(shape, jnp.float32),
            pltpu.SemaphoreType.DMA((NF,)),
            pltpu.VMEM(INVERSE, jnp.float32),
            TILES,
        ]
        + [pltpu.VMEM(STATE.shape, jnp.float32)] * 4
        + [
            pltpu.VMEM((NB, NB, 2, NF), jnp.float32),
            pltpu.SemaphoreType.DMA((NB,)),
        ],
        compiler_params=pltpu.CompilerParams(vmem_limit_bytes=24 << 20),
        name="finish",
    )(packed, ortho, first_real, first_imag)
    modes = modes.reshape(NF, NB, points // 128, 2, 128)
    modes = jnp.transpose(modes, (3, 0, 1, 2, 4)).reshape(2, NF, NB, points)
    return modes, jnp.transpose(triangle, (2, 3, 0, 1))


def shards(snapshots, weights):
    points_total = weights.shape[0] * lax.axis_size("tm") * lax.axis_size("pts")
    ortho, packed, *first = first_pass(snapshots, weights, points_total)
    return finish(packed, ortho, *first, points_total)


def solution(mesh):
    placed = (P("tm", "pts"), P(("pts", "tm")))
    return jax.shard_map(
        shards,
        mesh=mesh,
        in_specs=placed,
        out_specs=(P(None, None, None, ("pts", "tm")), P()),
        check_vma=False,
    )
```

```python
import math

import jax
import jax.numpy as jnp
import ml_dtypes
import numpy as np
from jax import lax
from jax.experimental import pallas as pl
from jax.experimental.pallas import tpu as pltpu
from jax.sharding import PartitionSpec as P

SEG = 64
HOP = 32
NF = 33
NT = 1024
NB = 31
MESH = pl.DeviceIdType.MESH

VMEM = pl.BlockSpec(memory_space=pltpu.VMEM)
TILE = 32
SLOTS = 32
LINES = SEG + 1
TILE_LINES = TILE + 1
SLOT_LINES = 41


def fourier_table():
    sample = np.arange(SEG)[:, None]
    column = np.arange(SEG)[None, :]
    frequency = np.where(column < NF, column, column - HOP)
    window = 0.5 - 0.5 * np.cos(2.0 * np.pi * sample / SEG)
    phase_angle = 2.0 * np.pi * ((frequency * sample) % SEG) / SEG
    waveform = np.where(column < NF, np.cos(phase_angle), -np.sin(phase_angle))
    return (waveform * window / np.sqrt(3 * SEG / 8)).astype(np.float32)


def table_parts():
    table = fourier_table().T
    high = table.astype(ml_dtypes.bfloat16)
    rest = table - high.astype(np.float32)
    middle = rest.astype(ml_dtypes.bfloat16)
    low = (rest - middle.astype(np.float32)).astype(ml_dtypes.bfloat16)
    return np.concatenate([high, high, middle, high, middle, low], axis=1)


def parts_of(value, count):
    parts = []
    for _ in range(count):
        part = value.astype(jnp.bfloat16)
        parts.append(part)
        value = value - part.astype(jnp.float32)
    return parts


def left6(value):
    high, middle, low = parts_of(value, 3)
    return jnp.concatenate([high, high, middle, high, middle, low], axis=1)


def right6(value):
    high, middle, low = parts_of(value, 3)
    return jnp.concatenate([high, middle, high, low, middle, high], axis=0)


def left3(value):
    high, low = parts_of(value, 2)
    return jnp.concatenate([high, high, low], axis=1)


def right3(value):
    high, low = parts_of(value, 2)
    return jnp.concatenate([high, low, high], axis=0)


def multiply(left, right):
    return jnp.dot(left, right, preferred_element_type=jnp.float32)


def self_product(value, count):
    stacked = jnp.concatenate(parts_of(value, count), axis=0)
    whole = lax.dot_general(
        stacked, stacked, (((1,), (1,)), ((), ())), preferred_element_type=jnp.float32
    )
    size = value.shape[0]
    rows = sum(whole[i * size : (i + 1) * size] for i in reversed(range(count)))
    return sum(rows[:, i * size : (i + 1) * size] for i in reversed(range(count)))


def gram_tile(product, slot):
    top_left = product[:TILE, :TILE]
    bottom_right = product[TILE:, TILE:]
    row = lax.broadcasted_iota(jnp.int32, (TILE, TILE), 0)
    column = lax.broadcasted_iota(jnp.int32, (TILE, TILE), 1)
    if slot == 0:
        return jnp.where(column >= row, top_left, pltpu.roll(bottom_right, 1, 0))
    imaginary = product[:TILE, TILE:] - product[TILE:, :TILE]
    return jnp.where(column >= row, top_left + bottom_right, imaginary)


def put_tiles(out, group, tiles, add):
    joined = jnp.concatenate(tiles, axis=1)
    if add:
        joined = joined + jnp.concatenate([out[2 * group], out[2 * group + 1]], axis=0)
    out[2 * group] = joined[:16]
    out[2 * group + 1] = joined[16:]


def slot_rows(spectrum, slot, panels):
    halves = [
        [
            spectrum[panel, pl.ds(slot + half, TILE, stride=LINES), :]
            for panel in panels
        ]
        for half in (0, 32)
    ]
    return jnp.concatenate([jnp.concatenate(row, axis=1) for row in halves], axis=0)


def remote(source, target, send, recv, device):
    return pltpu.make_async_remote_copy(
        src_ref=source, dst_ref=target, send_sem=send, recv_sem=recv,
        device_id=device, device_id_type=MESH,
    )


def all_of(ref, send, recv):
    me = lax.axis_index("tm")
    return remote(ref, ref, send, recv, {"tm": me + 1 - 2 * lax.rem(me, 2)})


def greet(device):
    pl.semaphore_signal(
        pltpu.get_barrier_semaphore(), inc=1, device_id=device, device_id_type=MESH
    )


def ring_offsets(n):
    return sorted(range(1, n), key=lambda d: -min(d, n - d))


def square_offsets(n):
    side = math.isqrt(n)
    offsets = [(i, j) for i in range(side) for j in range(side) if i or j]
    return sorted(
        offsets, key=lambda o: -(min(o[0], side - o[0]) + min(o[1], side - o[1]))
    )


def sum_stages(x_ref, o_ref, part, total, share, whole, *sems):
    send1, recv1, send2, recv2, send3, recv3 = sems
    me_p = lax.axis_index("pts")
    me_t = lax.axis_index("tm")
    core = lax.rem(me_t, 2)
    chip = me_t // 2
    n = part.shape[0] // 2
    side = math.isqrt(n)
    chips = share.shape[0]

    def lines(k):
        return pl.ds(pl.multiple_of(8 * k, 8), 8)

    own_lines = pl.ds(pl.multiple_of(16 * me_p + 8 * core, 8), 8)
    peers = [(i, j, c) for i, j in square_offsets(n) for c in (0, 1)] + [(0, 0, 1)]

    def peer(offset):
        i, j, c = offset
        row = lax.rem(me_p // side + i, side)
        to_p = row * side + lax.rem(lax.rem(me_p, side) + j, side)
        to_core = lax.rem(core + c, 2)
        device = {"pts": to_p, "tm": me_t - core + to_core}
        return device, to_p, to_core, (i * side + j) * 2 + c

    def scatter(offset):
        device, to_p, to_core, slot = peer(offset)
        return remote(
            x_ref.at[to_p, lines(to_core), :], part.at[slot], send1, recv1, device,
        )

    def exchange(d):
        to = {"tm": lax.rem(me_t + 2 * d, 2 * chips)}
        return remote(total, share.at[chip], send2, recv2, to)

    def gather(offset):
        device = peer(offset)[0]
        return remote(whole, o_ref.at[own_lines, :], send3, recv3, device)

    others = 2 * n - 1
    scattered = all_of(part.at[pl.ds(1, others)], send1, recv1)
    exchanged = all_of(share.at[pl.ds(0, chips - 1)], send2, recv2)
    gathered = all_of(o_ref.at[pl.ds(0, 8 * others), :], send3, recv3)
    for offset in peers:
        scatter(offset).start()
    part[0] = x_ref[me_p, lines(core), :]
    scattered.wait_recv()
    total[...] = jnp.sum(part[...], axis=0)
    for d in ring_offsets(chips):
        exchange(d).start()
    share[chip] = total[...]
    exchanged.wait_recv()
    whole[...] = jnp.sum(share[...], axis=0)
    for offset in peers:
        gather(offset).start()
    o_ref[own_lines, :] = whole[...]
    gathered.wait_recv()
    for stage in (scattered, exchanged, gathered):
        stage.wait_send()


def all_greetings():
    n = lax.axis_size("pts")
    side = math.isqrt(n)
    me_p = lax.axis_index("pts")
    me_t = lax.axis_index("tm")
    core = lax.rem(me_t, 2)
    chips = lax.axis_size("tm") // 2
    devices = [{"tm": lax.rem(me_t + 2 * d, 2 * chips)} for d in ring_offsets(chips)]
    for i, j in square_offsets(n):
        row = lax.rem(me_p // side + i, side)
        to_p = row * side + lax.rem(lax.rem(me_p, side) + j, side)
        devices.append({"pts": to_p})
        devices.append({"pts": to_p, "tm": me_t + 1 - 2 * core})
    devices.append({"tm": me_t + 1 - 2 * core})
    return devices


CHUNKS = (16, 16, 128)
SUMS = (256, 128)


def sum_scratch():
    n, lines, lanes = CHUNKS
    chips = lax.axis_size("tm") // 2
    dma = pltpu.SemaphoreType.DMA
    piece = (lines // 2, lanes)
    return [
        pltpu.VMEM((2 * n,) + piece, jnp.float32),
        pltpu.VMEM(piece, jnp.float32),
        pltpu.VMEM((chips,) + piece, jnp.float32),
        pltpu.VMEM(piece, jnp.float32),
    ] + [dma] * 6


def factor_lanes(scale, packed, tiles, state_real, state_imag):
    column = lax.broadcasted_iota(jnp.int32, (TILE, 128), 0)
    lane = lax.broadcasted_iota(jnp.int32, (TILE, 128), 1)
    for b in range(TILE):
        lines = packed[pl.ds(b, 8, stride=TILE), :]
        spread = jnp.concatenate(
            [lines] + [pltpu.roll(lines, 128 - 32 * s, 1) for s in (1, 2, 3)]
            + [jnp.zeros((96, 128), jnp.float32)],
            axis=0,
        )
        line = TILE_LINES * b
        tiles[line : line + TILE, :] = jnp.transpose(spread)[:TILE] * scale
    tiles[TILE * TILE_LINES :, :] = jnp.zeros((TILE, 128), jnp.float32)
    for b in range(NB):
        line = TILE_LINES * b
        straight = tiles[line : line + TILE, :]
        turned = tiles[pl.ds(b, TILE, stride=TILE_LINES), :]
        line = TILE_LINES * (b + 1)
        below = tiles[line : line + TILE, :]
        below_turned = tiles[pl.ds(TILE_LINES + b, TILE, stride=TILE_LINES), :]
        last = pltpu.roll(jnp.where(column <= b, below, below_turned), 32, 1)
        real = jnp.where(column >= b, straight, turned)
        real = jnp.where(lane == 32, last, real)
        imag = jnp.where(column < b, straight, -turned)
        state_real[b] = jnp.where(lane > 32, jnp.where(column == b, 1.0, 0.0), real)
        state_imag[b] = jnp.where(
            (lane == 0) | (lane >= 32) | (column == b), 0.0, imag
        )
    line = lax.broadcasted_iota(jnp.int32, (8, 128), 0)
    for k in range(NB):
        here = line == k % 8
        pivot = state_real[k, k : k + 1, :]
        inverse = lax.rsqrt(pivot)
        inverse = inverse * (1.5 - (0.5 * pivot * inverse) * inverse)
        rows = []
        for at in range(0, TILE, 8):
            group = slice(at, at + 8)
            real = state_real[k, group] * inverse
            imag = state_imag[k, group] * inverse
            if at == k // 8 * 8:
                real = jnp.where(here, inverse, real)
                imag = jnp.where(here, 0.0, imag)
            state_real[k, group] = real
            state_imag[k, group] = imag
            rows.append((real, imag))
        for i in range(k + 1, NB):
            pick_real = state_real[k, i : i + 1]
            pick_imag = state_imag[k, i : i + 1]
            for at in range(0, TILE, 8):
                if at > k and at + 7 < i:
                    continue
                group = slice(at, at + 8)
                real, imag = rows[at // 8]
                work_real = state_real[i, group]
                work_imag = state_imag[i, group]
                if at == k // 8 * 8:
                    work_real = jnp.where(here, 0.0, work_real)
                    work_imag = jnp.where(here, 0.0, work_imag)
                state_real[i, group] = work_real - (pick_real * real + pick_imag * imag)
                state_imag[i, group] = work_imag - (pick_real * imag - pick_imag * real)


def write_inverse(state_real, state_imag, inverse):
    column = lax.broadcasted_iota(jnp.int32, (TILE, 128), 0)
    lane = lax.broadcasted_iota(jnp.int32, (TILE, 128), 1)
    for k in range(NB):
        keep = column <= k
        real = jnp.where(keep, state_real[k], 0.0)
        imag = jnp.where(keep, state_imag[k], 0.0)
        lower = jnp.where(lane == 0, pltpu.roll(real, 96, 1), real)
        joined = jnp.concatenate([real, imag, -imag, lower], axis=0)
        line = SLOT_LINES * k
        inverse[line : line + SLOTS, :] = jnp.transpose(joined)[:SLOTS]
    line = SLOT_LINES * NB
    inverse[line : line + SLOTS, :] = jnp.zeros((SLOTS, 128), jnp.float32)


TILES = pltpu.VMEM((TILE * TILE_LINES + TILE, 128), jnp.float32)
STATE = jax.ShapeDtypeStruct((NB, TILE, 128), jnp.float32)
INVERSE = (TILE * SLOT_LINES, 128)


def slot_matrix(inverse, slot):
    lines = inverse[pl.ds(slot, TILE, stride=SLOT_LINES), :]
    return jnp.concatenate([lines[:, :64], lines[:, 64:]], axis=0)


PIECES = ((0, 384), (384, 128))


def first_kernel(
    points_total, snapshots, weights, table, ortho, result, state_real, state_imag,
    first, second, packed, parts, root, send, recv, own, spectrum, inverse, tiles, gathered,
    *sums,
):
    n = lax.axis_size("tm")
    me = lax.axis_index("tm")
    points = weights.shape[1]
    fetches = [
        pltpu.make_async_copy(table, parts, own.at[2]),
        pltpu.make_async_copy(weights, root, own.at[3]),
    ]
    for fetch in fetches:
        fetch.start()
    chips = n // 2
    core = lax.rem(me, 2)
    others = [(d, c) for d in ring_offsets(chips) for c in (0, 1)] + [(0, 1)]

    def other(offset):
        d, c = offset
        return lax.rem(me - core + 2 * d, n) + lax.rem(core + c, 2)

    for d in ring_offsets(chips):
        greet({"tm": other((d, 1))})
    devices = all_greetings()
    for device in devices:
        greet(device)
    greeted = len(devices) + chips - 1
    pl.semaphore_wait(pltpu.get_barrier_semaphore(), greeted)
    mine = pl.ds(pl.multiple_of(SEG * me, SEG), SEG)
    pieces = list(zip(range(2), PIECES, (first, second)))

    def column(device, start, width):
        return pl.ds(pl.multiple_of(device * points + start, 128), width)

    def travel(piece, offset):
        index, (start, width), target = piece
        to = other(offset)
        return remote(
            snapshots.at[:, column(to, start, width)],
            target.at[mine, :],
            send.at[index],
            recv.at[index],
            {"tm": to},
        )

    def arrived(piece):
        index, _, target = piece
        lines = target.at[pl.ds(0, SEG * (n - 1)), :]
        return all_of(lines, send.at[index], recv.at[index])

    def stay(piece):
        index, (start, width), target = piece
        return pltpu.make_async_copy(
            snapshots.at[:, column(me, start, width)], target.at[mine, :], own.at[index]
        )

    for piece in pieces:
        for offset in others:
            travel(piece, offset).start()
        stay(piece).start()
    for fetch in fetches:
        fetch.wait()
    for panel in range(spectrum.shape[0]):
        spectrum[panel, NB * LINES :, :] = jnp.zeros((LINES, 128), jnp.float32)
    for piece in pieces:
        index, (start, width), target = piece
        stay(piece).wait()
        arrived(piece).wait_recv()
        panels = range(start // 128, (start + width) // 128)
        scale = jnp.sqrt(root[:, start : start + width])

        for b in range(NB):
            rows = target[HOP * b : HOP * b + SEG, :]
            value = multiply(parts[...], right6(rows)) * scale
            for panel in panels:
                at = 128 * panel - start
                spectrum[panel, LINES * b : LINES * b + SEG, :] = value[:, at : at + 128]
        for group in range(8):
            products = [
                gram_tile(self_product(slot_rows(spectrum, slot, panels), 3), slot)
                for slot in range(group, SLOTS, 8)
            ]
            put_tiles(packed, group, products, index > 0)
    half = len(sums) // 2
    sum_stages(packed, gathered, *sums[:half])
    factor_lanes(1.0 / points_total, gathered, tiles, state_real, state_imag)
    write_inverse(state_real, state_imag, inverse)
    for slot in range(SLOTS):
        value = slot_rows(spectrum, slot, range(spectrum.shape[0]))
        ortho[slot] = multiply(left6(slot_matrix(inverse, slot)), right6(value))
    for group in range(8):
        products = [
            gram_tile(self_product(ortho[slot], 2), slot)
            for slot in range(group, SLOTS, 8)
        ]
        put_tiles(packed, group, products, False)
    sum_stages(packed, result, *sums[half:])
    for piece in pieces:
        arrived(piece).wait_send()


def first_pass(snapshots, weights, points_total):
    points = weights.shape[0]
    n = lax.axis_size("tm")
    dma = pltpu.SemaphoreType.DMA
    inputs = (snapshots, weights.reshape(1, points), jnp.asarray(table_parts()))
    return pl.pallas_call(
        lambda *refs: first_kernel(points_total, *refs),
        out_shape=(
            jax.ShapeDtypeStruct((SLOTS, SEG, points), jnp.float32),
            jax.ShapeDtypeStruct(SUMS, jnp.float32),
            STATE,
            STATE,
        ),
        in_specs=[pl.BlockSpec(memory_space=pltpu.HBM)] * 3,
        out_specs=(VMEM,) * 4,
        scratch_shapes=[pltpu.VMEM((NT, width), jnp.float32) for _, width in PIECES]
        + [
            pltpu.VMEM(CHUNKS, jnp.float32),
            pltpu.VMEM((SEG, 6 * SEG), jnp.bfloat16),
            pltpu.VMEM((1, points), jnp.float32),
            dma((2,)),
            dma((2,)),
            dma((4,)),
            pltpu.VMEM((points // 128, TILE * LINES, 128), jnp.float32),
            pltpu.VMEM(INVERSE, jnp.float32),
            TILES,
            pltpu.VMEM(SUMS, jnp.float32),
        ]
        + sum_scratch() * 2,
        compiler_params=pltpu.CompilerParams(
            vmem_limit_bytes=32 << 20, collective_id=0, has_side_effects=True
        ),
        name="first_pass",
    )(*(pltpu.with_memory_space_constraint(x, pltpu.HBM) for x in inputs))


def send_modes(ortho, inverse, modes, held, sems):
    copies = []
    panels = ortho.shape[2] // 128
    step = 2 * panels

    def put(frequency, part, value):
        for panel in range(panels):
            held[frequency, pl.ds(2 * panel + part, NB, stride=step), :] = value[
                :NB, 128 * panel : 128 * (panel + 1)
            ]

    def send(frequency):
        copy = pltpu.make_async_copy(
            held.at[frequency], modes.at[frequency], sems.at[frequency]
        )
        copy.start()
        copies.append(copy)

    for slot in range(SLOTS):
        value = multiply(left3(slot_matrix(inverse, slot)), right3(ortho[slot]))
        put(slot, 0, value[:TILE])
        if slot:
            put(slot, 1, value[TILE:])
        else:
            nothing = jnp.zeros((TILE, value.shape[1]), jnp.float32)
            put(0, 1, nothing)
            put(NF - 1, 0, value[TILE:])
            put(NF - 1, 1, nothing)
            send(NF - 1)
        send(slot)
    return copies


def finish_kernel(
    scale, packed, ortho, first_real, first_imag, modes, triangle,
    held, sems, inverse, tiles, state_real, state_imag, right_real, right_imag, rows, row_sems,
):
    factor_lanes(scale, packed, tiles, state_real, state_imag)
    write_inverse(state_real, state_imag, inverse)
    copies = send_modes(ortho, inverse, modes, held, sems)
    column = lax.broadcasted_iota(jnp.int32, (TILE, 128), 0)
    for k in range(NB):
        real = first_real[k]
        diagonal = jnp.where(column == k, 1.0 / real, 0.0)
        right_real[k] = jnp.where(column > k, real, diagonal)
        right_imag[k] = jnp.where(column > k, first_imag[k], 0.0)
    for i in range(NB):
        first = i // 8 * 8
        own = 1.0 / state_real[i, i : i + 1, :]
        groups = range(first, TILE, 8)
        total_real = {at: own * right_real[i, at : at + 8] for at in groups}
        total_imag = {at: own * right_imag[i, at : at + 8] for at in groups}
        for k in range(i + 1, NB):
            pick_real = state_real[i, k : k + 1]
            pick_imag = state_imag[i, k : k + 1]
            for at in range(k // 8 * 8, TILE, 8):
                real = right_real[k, at : at + 8]
                imag = right_imag[k, at : at + 8]
                total_real[at] = total_real[at] + (pick_real * real - pick_imag * imag)
                total_imag[at] = total_imag[at] + (pick_real * imag + pick_imag * real)
        for part, total in enumerate((total_real, total_imag)):
            zeros = [jnp.zeros((8, 128), jnp.float32)] * (first // 8)
            line = jnp.concatenate(zeros + [total[at] for at in groups], axis=0)
            rows[i, :, part, :] = line[:NB, :NF]
        copy = pltpu.make_async_copy(rows.at[i], triangle.at[i], row_sems.at[i])
        copy.start()
        copies.append(copy)
    for copy in copies:
        copy.wait()


def finish(packed, ortho, first_real, first_imag, points_total):
    points = ortho.shape[2]
    shape = (NF, NB * points // 64, 128)
    modes, triangle = pl.pallas_call(
        lambda *refs: finish_kernel(1.0 / points_total, *refs),
        out_shape=(
            jax.ShapeDtypeStruct(shape, jnp.float32),
            jax.ShapeDtypeStruct((NB, NB, 2, NF), jnp.float32),
        ),
        in_specs=[VMEM] * 4,
        out_specs=(pl.BlockSpec(memory_space=pl.ANY),) * 2,
        scratch_shapes=[
            pltpu.VMEM(shape, jnp.float32),
            pltpu.SemaphoreType.DMA((NF,)),
            pltpu.VMEM(INVERSE, jnp.float32),
            TILES,
        ]
        + [pltpu.VMEM(STATE.shape, jnp.float32)] * 4
        + [
            pltpu.VMEM((NB, NB, 2, NF), jnp.float32),
            pltpu.SemaphoreType.DMA((NB,)),
        ],
        compiler_params=pltpu.CompilerParams(vmem_limit_bytes=24 << 20),
        name="finish",
    )(packed, ortho, first_real, first_imag)
    modes = modes.reshape(NF, NB, points // 128, 2, 128)
    modes = jnp.transpose(modes, (3, 0, 1, 2, 4)).reshape(2, NF, NB, points)
    return modes, jnp.transpose(triangle, (2, 3, 0, 1))


def shards(snapshots, weights):
    points_total = weights.shape[0] * lax.axis_size("tm") * lax.axis_size("pts")
    ortho, packed, *first = first_pass(snapshots, weights, points_total)
    return finish(packed, ortho, *first, points_total)


def solution(mesh):
    placed = (P("tm", "pts"), P(("pts", "tm")))
    return jax.shard_map(
        shards,
        mesh=mesh,
        in_specs=placed,
        out_specs=(P(None, None, None, ("pts", "tm")), P()),
        check_vma=False,
    )
```

```python
import math

import jax
import jax.numpy as jnp
import ml_dtypes
import numpy as np
from jax import lax
from jax.experimental import pallas as pl
from jax.experimental.pallas import tpu as pltpu
from jax.sharding import PartitionSpec as P

SEG = 64
HOP = 32
NF = 33
NT = 1024
NB = 31
MESH = pl.DeviceIdType.MESH

VMEM = pl.BlockSpec(memory_space=pltpu.VMEM)
TILE = 32
SLOTS = 32
LINES = SEG + 1
TILE_LINES = TILE + 1
SLOT_LINES = 41


def fourier_table():
    sample = np.arange(SEG)[:, None]
    column = np.arange(SEG)[None, :]
    frequency = np.where(column < NF, column, column - HOP)
    window = 0.5 - 0.5 * np.cos(2.0 * np.pi * sample / SEG)
    phase_angle = 2.0 * np.pi * ((frequency * sample) % SEG) / SEG
    waveform = np.where(column < NF, np.cos(phase_angle), -np.sin(phase_angle))
    return (waveform * window / np.sqrt(3 * SEG / 8)).astype(np.float32)


def table_parts():
    table = fourier_table().T
    high = table.astype(ml_dtypes.bfloat16)
    rest = table - high.astype(np.float32)
    middle = rest.astype(ml_dtypes.bfloat16)
    low = (rest - middle.astype(np.float32)).astype(ml_dtypes.bfloat16)
    return np.concatenate([high, high, middle, high, middle, low], axis=1)


def parts_of(value, count):
    parts = []
    for _ in range(count):
        part = value.astype(jnp.bfloat16)
        parts.append(part)
        value = value - part.astype(jnp.float32)
    return parts


def left6(value):
    high, middle, low = parts_of(value, 3)
    return jnp.concatenate([high, high, middle, high, middle, low], axis=1)


def right6(value):
    high, middle, low = parts_of(value, 3)
    return jnp.concatenate([high, middle, high, low, middle, high], axis=0)


def left3(value):
    high, low = parts_of(value, 2)
    return jnp.concatenate([high, high, low], axis=1)


def right3(value):
    high, low = parts_of(value, 2)
    return jnp.concatenate([high, low, high], axis=0)


def multiply(left, right):
    return jnp.dot(left, right, preferred_element_type=jnp.float32)


def self_product(value, count):
    stacked = jnp.concatenate(parts_of(value, count), axis=0)
    whole = lax.dot_general(
        stacked, stacked, (((1,), (1,)), ((), ())), preferred_element_type=jnp.float32
    )
    size = value.shape[0]
    rows = sum(whole[i * size : (i + 1) * size] for i in reversed(range(count)))
    return sum(rows[:, i * size : (i + 1) * size] for i in reversed(range(count)))


def gram_tile(product, slot):
    top_left = product[:TILE, :TILE]
    bottom_right = product[TILE:, TILE:]
    row = lax.broadcasted_iota(jnp.int32, (TILE, TILE), 0)
    column = lax.broadcasted_iota(jnp.int32, (TILE, TILE), 1)
    if slot == 0:
        return jnp.where(column >= row, top_left, pltpu.roll(bottom_right, 1, 0))
    imaginary = product[:TILE, TILE:] - product[TILE:, :TILE]
    return jnp.where(column >= row, top_left + bottom_right, imaginary)


def put_tiles(out, group, tiles, add):
    joined = jnp.concatenate(tiles, axis=1)
    if add:
        joined = joined + jnp.concatenate([out[2 * group], out[2 * group + 1]], axis=0)
    out[2 * group] = joined[:16]
    out[2 * group + 1] = joined[16:]


def slot_rows(spectrum, slot, panels):
    halves = [
        [
            spectrum[panel, pl.ds(slot + half, TILE, stride=LINES), :]
            for panel in panels
        ]
        for half in (0, 32)
    ]
    return jnp.concatenate([jnp.concatenate(row, axis=1) for row in halves], axis=0)


def remote(source, target, send, recv, device):
    return pltpu.make_async_remote_copy(
        src_ref=source, dst_ref=target, send_sem=send, recv_sem=recv,
        device_id=device, device_id_type=MESH,
    )


def all_of(ref, send, recv):
    me = lax.axis_index("tm")
    return remote(ref, ref, send, recv, {"tm": me + 1 - 2 * lax.rem(me, 2)})


def greet(device):
    pl.semaphore_signal(
        pltpu.get_barrier_semaphore(), inc=1, device_id=device, device_id_type=MESH
    )


def ring_offsets(n):
    return sorted(range(1, n), key=lambda d: -min(d, n - d))


def square_offsets(n):
    side = math.isqrt(n)
    offsets = [(i, j) for i in range(side) for j in range(side) if i or j]
    return sorted(
        offsets, key=lambda o: -(min(o[0], side - o[0]) + min(o[1], side - o[1]))
    )


def sum_stages(x_ref, o_ref, part, total, share, whole, *sems):
    send1, recv1, send2, recv2, send3, recv3 = sems
    me_p = lax.axis_index("pts")
    me_t = lax.axis_index("tm")
    core = lax.rem(me_t, 2)
    chip = me_t // 2
    n = part.shape[0] // 2
    side = math.isqrt(n)
    chips = share.shape[0]

    def lines(k):
        return pl.ds(pl.multiple_of(8 * k, 8), 8)

    own_lines = pl.ds(pl.multiple_of(16 * me_p + 8 * core, 8), 8)
    peers = [(i, j, c) for i, j in square_offsets(n) for c in (0, 1)] + [(0, 0, 1)]

    def peer(offset):
        i, j, c = offset
        row = lax.rem(me_p // side + i, side)
        to_p = row * side + lax.rem(lax.rem(me_p, side) + j, side)
        to_core = lax.rem(core + c, 2)
        device = {"pts": to_p, "tm": me_t - core + to_core}
        return device, to_p, to_core, (i * side + j) * 2 + c

    def scatter(offset):
        device, to_p, to_core, slot = peer(offset)
        return remote(
            x_ref.at[to_p, lines(to_core), :], part.at[slot], send1, recv1, device,
        )

    def exchange(d):
        to = {"tm": lax.rem(me_t + 2 * d, 2 * chips)}
        return remote(total, share.at[chip], send2, recv2, to)

    def gather(offset):
        device = peer(offset)[0]
        return remote(whole, o_ref.at[own_lines, :], send3, recv3, device)

    others = 2 * n - 1
    scattered = all_of(part.at[pl.ds(1, others)], send1, recv1)
    exchanged = all_of(share.at[pl.ds(0, chips - 1)], send2, recv2)
    gathered = all_of(o_ref.at[pl.ds(0, 8 * others), :], send3, recv3)
    for offset in peers:
        scatter(offset).start()
    part[0] = x_ref[me_p, lines(core), :]
    scattered.wait_recv()
    total[...] = jnp.sum(part[...], axis=0)
    for d in ring_offsets(chips):
        exchange(d).start()
    share[chip] = total[...]
    exchanged.wait_recv()
    whole[...] = jnp.sum(share[...], axis=0)
    for offset in peers:
        gather(offset).start()
    o_ref[own_lines, :] = whole[...]
    gathered.wait_recv()
    for stage in (scattered, exchanged, gathered):
        stage.wait_send()


def all_greetings():
    n = lax.axis_size("pts")
    side = math.isqrt(n)
    me_p = lax.axis_index("pts")
    me_t = lax.axis_index("tm")
    core = lax.rem(me_t, 2)
    chips = lax.axis_size("tm") // 2
    devices = [{"tm": lax.rem(me_t + 2 * d, 2 * chips)} for d in ring_offsets(chips)]
    for i, j in square_offsets(n):
        row = lax.rem(me_p // side + i, side)
        to_p = row * side + lax.rem(lax.rem(me_p, side) + j, side)
        devices.append({"pts": to_p})
        devices.append({"pts": to_p, "tm": me_t + 1 - 2 * core})
    devices.append({"tm": me_t + 1 - 2 * core})
    return devices


CHUNKS = (16, 16, 128)
SUMS = (256, 128)


def sum_scratch():
    n, lines, lanes = CHUNKS
    chips = lax.axis_size("tm") // 2
    dma = pltpu.SemaphoreType.DMA
    piece = (lines // 2, lanes)
    return [
        pltpu.VMEM((2 * n,) + piece, jnp.float32),
        pltpu.VMEM(piece, jnp.float32),
        pltpu.VMEM((chips,) + piece, jnp.float32),
        pltpu.VMEM(piece, jnp.float32),
    ] + [dma] * 6


def factor_lanes(scale, packed, tiles, state_real, state_imag):
    column = lax.broadcasted_iota(jnp.int32, (TILE, 128), 0)
    lane = lax.broadcasted_iota(jnp.int32, (TILE, 128), 1)
    for b in range(TILE):
        lines = packed[pl.ds(b, 8, stride=TILE), :]
        spread = jnp.concatenate(
            [lines] + [pltpu.roll(lines, 128 - 32 * s, 1) for s in (1, 2, 3)]
            + [jnp.zeros((96, 128), jnp.float32)],
            axis=0,
        )
        line = TILE_LINES * b
        tiles[line : line + TILE, :] = jnp.transpose(spread)[:TILE] * scale
    tiles[TILE * TILE_LINES :, :] = jnp.zeros((TILE, 128), jnp.float32)
    for b in range(NB):
        line = TILE_LINES * b
        straight = tiles[line : line + TILE, :]
        turned = tiles[pl.ds(b, TILE, stride=TILE_LINES), :]
        line = TILE_LINES * (b + 1)
        below = tiles[line : line + TILE, :]
        below_turned = tiles[pl.ds(TILE_LINES + b, TILE, stride=TILE_LINES), :]
        last = pltpu.roll(jnp.where(column <= b, below, below_turned), 32, 1)
        real = jnp.where(column >= b, straight, turned)
        real = jnp.where(lane == 32, last, real)
        imag = jnp.where(column < b, straight, -turned)
        state_real[b] = jnp.where(lane > 32, jnp.where(column == b, 1.0, 0.0), real)
        state_imag[b] = jnp.where(
            (lane == 0) | (lane >= 32) | (column == b), 0.0, imag
        )
    line = lax.broadcasted_iota(jnp.int32, (8, 128), 0)
    for k in range(NB):
        here = line == k % 8
        pivot = state_real[k, k : k + 1, :]
        inverse = lax.rsqrt(pivot)
        inverse = inverse * (1.5 - (0.5 * pivot * inverse) * inverse)
        rows = []
        for at in range(0, TILE, 8):
            group = slice(at, at + 8)
            real = state_real[k, group] * inverse
            imag = state_imag[k, group] * inverse
            if at == k // 8 * 8:
                real = jnp.where(here, inverse, real)
                imag = jnp.where(here, 0.0, imag)
            state_real[k, group] = real
            state_imag[k, group] = imag
            rows.append((real, imag))
        for i in range(k + 1, NB):
            pick_real = state_real[k, i : i + 1]
            pick_imag = state_imag[k, i : i + 1]
            for at in range(0, TILE, 8):
                if at > k and at + 7 < i:
                    continue
                group = slice(at, at + 8)
                real, imag = rows[at // 8]
                work_real = state_real[i, group]
                work_imag = state_imag[i, group]
                if at == k // 8 * 8:
                    work_real = jnp.where(here, 0.0, work_real)
                    work_imag = jnp.where(here, 0.0, work_imag)
                state_real[i, group] = work_real - (pick_real * real + pick_imag * imag)
                state_imag[i, group] = work_imag - (pick_real * imag - pick_imag * real)


def write_inverse(state_real, state_imag, inverse):
    column = lax.broadcasted_iota(jnp.int32, (TILE, 128), 0)
    lane = lax.broadcasted_iota(jnp.int32, (TILE, 128), 1)
    for k in range(NB):
        keep = column <= k
        real = jnp.where(keep, state_real[k], 0.0)
        imag = jnp.where(keep, state_imag[k], 0.0)
        lower = jnp.where(lane == 0, pltpu.roll(real, 96, 1), real)
        joined = jnp.concatenate([real, imag, -imag, lower], axis=0)
        line = SLOT_LINES * k
        inverse[line : line + SLOTS, :] = jnp.transpose(joined)[:SLOTS]
    line = SLOT_LINES * NB
    inverse[line : line + SLOTS, :] = jnp.zeros((SLOTS, 128), jnp.float32)


TILES = pltpu.VMEM((TILE * TILE_LINES + TILE, 128), jnp.float32)
STATE = jax.ShapeDtypeStruct((NB, TILE, 128), jnp.float32)
INVERSE = (TILE * SLOT_LINES, 128)


def slot_matrix(inverse, slot):
    lines = inverse[pl.ds(slot, TILE, stride=SLOT_LINES), :]
    return jnp.concatenate([lines[:, :64], lines[:, 64:]], axis=0)


PIECES = ((0, 384), (384, 128))


def first_kernel(
    points_total, snapshots, weights, table, ortho, result, state_real, state_imag,
    first, second, packed, parts, root, send, recv, own, spectrum, inverse, tiles, gathered,
    *sums,
):
    n = lax.axis_size("tm")
    me = lax.axis_index("tm")
    points = weights.shape[1]
    fetches = [
        pltpu.make_async_copy(table, parts, own.at[2]),
        pltpu.make_async_copy(weights, root, own.at[3]),
    ]
    for fetch in fetches:
        fetch.start()
    chips = n // 2
    core = lax.rem(me, 2)
    others = [(d, c) for d in ring_offsets(chips) for c in (0, 1)] + [(0, 1)]

    def other(offset):
        d, c = offset
        return lax.rem(me - core + 2 * d, n) + lax.rem(core + c, 2)

    for d in ring_offsets(chips):
        greet({"tm": other((d, 1))})
    devices = all_greetings()
    for device in devices:
        greet(device)
    greeted = len(devices) + chips - 1
    pl.semaphore_wait(pltpu.get_barrier_semaphore(), greeted)
    mine = pl.ds(pl.multiple_of(SEG * me, SEG), SEG)
    pieces = list(zip(range(2), PIECES, (first, second)))

    def column(device, start, width):
        return pl.ds(pl.multiple_of(device * points + start, 128), width)

    def travel(piece, offset):
        index, (start, width), target = piece
        to = other(offset)
        return remote(
            snapshots.at[:, column(to, start, width)],
            target.at[mine, :],
            send.at[index],
            recv.at[index],
            {"tm": to},
        )

    def arrived(piece):
        index, _, target = piece
        lines = target.at[pl.ds(0, SEG * (n - 1)), :]
        return all_of(lines, send.at[index], recv.at[index])

    def stay(piece):
        index, (start, width), target = piece
        return pltpu.make_async_copy(
            snapshots.at[:, column(me, start, width)], target.at[mine, :], own.at[index]
        )

    for piece in pieces:
        for offset in others:
            travel(piece, offset).start()
        stay(piece).start()
    for fetch in fetches:
        fetch.wait()
    for panel in range(spectrum.shape[0]):
        spectrum[panel, NB * LINES :, :] = jnp.zeros((LINES, 128), jnp.float32)
    for piece in pieces:
        index, (start, width), target = piece
        stay(piece).wait()
        arrived(piece).wait_recv()
        panels = range(start // 128, (start + width) // 128)
        scale = jnp.sqrt(root[:, start : start + width])

        for b in range(NB):
            rows = target[HOP * b : HOP * b + SEG, :]
            value = multiply(parts[...], right6(rows)) * scale
            for panel in panels:
                at = 128 * panel - start
                spectrum[panel, LINES * b : LINES * b + SEG, :] = value[:, at : at + 128]
        for group in range(8):
            products = [
                gram_tile(self_product(slot_rows(spectrum, slot, panels), 3), slot)
                for slot in range(group, SLOTS, 8)
            ]
            put_tiles(packed, group, products, index > 0)
    half = len(sums) // 2
    sum_stages(packed, gathered, *sums[:half])
    factor_lanes(1.0 / points_total, gathered, tiles, state_real, state_imag)
    write_inverse(state_real, state_imag, inverse)
    for slot in range(SLOTS):
        value = slot_rows(spectrum, slot, range(spectrum.shape[0]))
        ortho[slot] = multiply(left6(slot_matrix(inverse, slot)), right6(value))
    for group in range(8):
        products = [
            gram_tile(self_product(ortho[slot], 2), slot)
            for slot in range(group, SLOTS, 8)
        ]
        put_tiles(packed, group, products, False)
    sum_stages(packed, result, *sums[half:])
    for piece in pieces:
        arrived(piece).wait_send()


def first_pass(snapshots, weights, points_total):
    points = weights.shape[0]
    n = lax.axis_size("tm")
    dma = pltpu.SemaphoreType.DMA
    inputs = (snapshots, weights.reshape(1, points), jnp.asarray(table_parts()))
    return pl.pallas_call(
        lambda *refs: first_kernel(points_total, *refs),
        out_shape=(
            jax.ShapeDtypeStruct((SLOTS, SEG, points), jnp.float32),
            jax.ShapeDtypeStruct(SUMS, jnp.float32),
            STATE,
            STATE,
        ),
        in_specs=[pl.BlockSpec(memory_space=pltpu.HBM)] * 3,
        out_specs=(VMEM,) * 4,
        scratch_shapes=[pltpu.VMEM((NT, width), jnp.float32) for _, width in PIECES]
        + [
            pltpu.VMEM(CHUNKS, jnp.float32),
            pltpu.VMEM((SEG, 6 * SEG), jnp.bfloat16),
            pltpu.VMEM((1, points), jnp.float32),
            dma((2,)),
            dma((2,)),
            dma((4,)),
            pltpu.VMEM((points // 128, TILE * LINES, 128), jnp.float32),
            pltpu.VMEM(INVERSE, jnp.float32),
            TILES,
            pltpu.VMEM(SUMS, jnp.float32),
        ]
        + sum_scratch() * 2,
        compiler_params=pltpu.CompilerParams(
            vmem_limit_bytes=32 << 20, collective_id=0, has_side_effects=True
        ),
        name="first_pass",
    )(*(pltpu.with_memory_space_constraint(x, pltpu.HBM) for x in inputs))


def send_modes(ortho, inverse, modes, held, sem):
    panels = ortho.shape[2] // 128
    step = 2 * panels

    def put(frequency, part, value):
        for panel in range(panels):
            held[frequency, pl.ds(2 * panel + part, NB, stride=step), :] = value[
                :NB, 128 * panel : 128 * (panel + 1)
            ]

    def send(frequency):
        pltpu.make_async_copy(held.at[frequency], modes.at[frequency], sem).start()

    for slot in range(SLOTS):
        value = multiply(left3(slot_matrix(inverse, slot)), right3(ortho[slot]))
        put(slot, 0, value[:TILE])
        if slot:
            put(slot, 1, value[TILE:])
        else:
            nothing = jnp.zeros((TILE, value.shape[1]), jnp.float32)
            put(0, 1, nothing)
            put(NF - 1, 0, value[TILE:])
            put(NF - 1, 1, nothing)
            send(NF - 1)
        send(slot)


def finish_kernel(
    scale, packed, ortho, first_real, first_imag, modes, triangle,
    held, sem, inverse, tiles, state_real, state_imag, right_real, right_imag, rows, row_sem,
):
    factor_lanes(scale, packed, tiles, state_real, state_imag)
    write_inverse(state_real, state_imag, inverse)
    send_modes(ortho, inverse, modes, held, sem)
    column = lax.broadcasted_iota(jnp.int32, (TILE, 128), 0)
    for k in range(NB):
        real = first_real[k]
        diagonal = jnp.where(column == k, 1.0 / real, 0.0)
        right_real[k] = jnp.where(column > k, real, diagonal)
        right_imag[k] = jnp.where(column > k, first_imag[k], 0.0)
    for i in range(NB):
        first = i // 8 * 8
        own = 1.0 / state_real[i, i : i + 1, :]
        groups = range(first, TILE, 8)
        total_real = {at: own * right_real[i, at : at + 8] for at in groups}
        total_imag = {at: own * right_imag[i, at : at + 8] for at in groups}
        for k in range(i + 1, NB):
            pick_real = state_real[i, k : k + 1]
            pick_imag = state_imag[i, k : k + 1]
            for at in range(k // 8 * 8, TILE, 8):
                real = right_real[k, at : at + 8]
                imag = right_imag[k, at : at + 8]
                total_real[at] = total_real[at] + (pick_real * real - pick_imag * imag)
                total_imag[at] = total_imag[at] + (pick_real * imag + pick_imag * real)
        for part, total in enumerate((total_real, total_imag)):
            zeros = [jnp.zeros((8, 128), jnp.float32)] * (first // 8)
            line = jnp.concatenate(zeros + [total[at] for at in groups], axis=0)
            rows[i, :, part, :] = line[:NB, :NF]
        pltpu.make_async_copy(rows.at[i], triangle.at[i], row_sem).start()
    pltpu.make_async_copy(held, modes, sem).wait()
    pltpu.make_async_copy(rows, triangle, row_sem).wait()


def finish(packed, ortho, first_real, first_imag, points_total):
    points = ortho.shape[2]
    shape = (NF, NB * points // 64, 128)
    modes, triangle = pl.pallas_call(
        lambda *refs: finish_kernel(1.0 / points_total, *refs),
        out_shape=(
            jax.ShapeDtypeStruct(shape, jnp.float32),
            jax.ShapeDtypeStruct((NB, NB, 2, NF), jnp.float32),
        ),
        in_specs=[VMEM] * 4,
        out_specs=(pl.BlockSpec(memory_space=pl.ANY),) * 2,
        scratch_shapes=[
            pltpu.VMEM(shape, jnp.float32),
            pltpu.SemaphoreType.DMA,
            pltpu.VMEM(INVERSE, jnp.float32),
            TILES,
        ]
        + [pltpu.VMEM(STATE.shape, jnp.float32)] * 4
        + [
            pltpu.VMEM((NB, NB, 2, NF), jnp.float32),
            pltpu.SemaphoreType.DMA,
        ],
        compiler_params=pltpu.CompilerParams(vmem_limit_bytes=24 << 20),
        name="finish",
    )(packed, ortho, first_real, first_imag)
    modes = modes.reshape(NF, NB, points // 128, 2, 128)
    modes = jnp.transpose(modes, (3, 0, 1, 2, 4)).reshape(2, NF, NB, points)
    return modes, jnp.transpose(triangle, (2, 3, 0, 1))


def shards(snapshots, weights):
    points_total = weights.shape[0] * lax.axis_size("tm") * lax.axis_size("pts")
    ortho, packed, *first = first_pass(snapshots, weights, points_total)
    return finish(packed, ortho, *first, points_total)


def solution(mesh):
    placed = (P("tm", "pts"), P(("pts", "tm")))
    return jax.shard_map(
        shards,
        mesh=mesh,
        in_specs=placed,
        out_specs=(P(None, None, None, ("pts", "tm")), P()),
        check_vma=False,
    )
```
